32 devices in a mesh: grp: 2 (over y), lab: 4 (over z), dp: 2 (over x), sub: 2 (over core).
Axes of the slice: x: 2, y: 2, z: 4, core: 2. Of those that a mesh axis runs over, the one named last changes fastest.
Arguments:
- enc_rows: bfloat16 [4096, 2048], P(('grp', 'lab', 'dp'), 'sub'), parts along dimension 0, may hold values from -6 to 6
- shortlist: int32 [4096, 8], P(('grp', 'lab', 'dp')), parts along dimension 0, may hold values from 0 to 15, all different within a row; in each aligned block of 256 rows (0 to 255, 256 to 511, ...) at most 256 rows name the same one
- cluster_slot: int32 [16], replicated, may hold values from 0 to 15, each once
- positives: int32 [4096, 16], P(('grp', 'lab', 'dp')), parts along dimension 0, may hold values from 0 to 2047
- panels: bfloat16 [16, 2048, 256], P('lab', 'sub'), may hold values from -0.125 to 0.125
Outputs:
- enc_grad: bfloat16 [4096, 2048], P(('grp', 'lab', 'dp'), 'sub'), parts along dimension 0
- panel_grad: float32 [32, 2048, 256], P(('grp', 'lab', 'dp'), 'sub'), parts along dimension 0
The draws below stay inside these ranges and needn't reach their ends.
There are 2 independent parts, one for each index of `grp`. The reference program is written for one: setup_inputs(seed, part) draws one part's arguments, and reference() takes and returns one part's arrays. A program takes and returns all parts, laid end to end along the dimension named above; an argument that names none is the same for every part. Nothing has to cross between parts.
Inputs may be any that keep to these rules, and one draw needn't show every extreme that they name: `shortlist`: each sample names 8 different clusters. Among the 256 samples of one device (aligned blocks of rows, in order), no cluster is named more than 256 times; in some such blocks a cluster is named exactly 256 times. `cluster_slot`: each panel index occurs once. `positives`: A value v stands for label v % 256 of the sample's shortlisted cluster number v // 256; values may repeat.
All inputs are finite; a program needn't handle non-finite values.
Results may differ from the reference program's by a relative error of at most 0.011.
Values may be sent and summed in bfloat16 or wider, within the bound.
A program may use at most 128 MiB of HBM per device.

```python
import math
import jax
import jax.numpy as jnp
import numpy as np
from jax import lax

H = 2048
B = 256
K = 8
P_SIZE = 16
S_DEV = 256
SAMPLES = 2048
CLUSTERS = 16
MOST = 256


def place_ends(drawn, own_key, low, high):
    extent = drawn.shape
    spot = [jax.random.randint(jax.random.fold_in(own_key, axis), (), 0, extent[axis]) for axis in range(len(extent))]
    drawn = drawn.at[tuple(spot)].set(low)
    longest = extent.index(max(extent))
    spot[longest] = (spot[longest] + 1) % extent[longest]
    return drawn.at[tuple(spot)].set(high)


def block_levels(key, extent, split, least, top_value):
    def one(dim, blocks):
        draws = jax.random.uniform(jax.random.fold_in(jax.random.fold_in(key, 6), dim), (blocks,), jnp.float32, least / len(split), top_value / len(split))
        return jnp.repeat(jnp.exp(draws), extent[dim] // blocks).reshape((-1,) + (1,) * (len(extent) - dim - 1))

    loudness = one(*split[0])
    for cut in split[1:]:
        loudness = loudness * one(*cut)
    return loudness


def assign_block(rng, own, number, rows, number_of, top, limit, skew):
    sequence = jax.random.permutation(rng, number_of)
    crowded, common = portions_of(number_of, rows * top, limit, skew, True), portions_of(number_of, rows * top, limit, skew, False)
    places = jnp.arange(number_of)

    def named(lengths, rotation):
        used = int((lengths > 0).sum())
        fixed = max(1, used // 4)
        moved = fixed + (places - fixed + rotation * (used - fixed)) % max(1, number_of - fixed)
        return jnp.zeros((number_of,), jnp.int32).at[sequence[jnp.where(places < fixed, places, moved)]].set(jnp.asarray(lengths, jnp.int32))

    lengths = jnp.where(number % 4 == 0, named(crowded, number // 4), named(common, number - number // 4 - 1))
    mixed = jax.random.permutation(jax.random.fold_in(own, 3), number_of)
    donor, sink = mixed[0:number_of // 2 * 2:2], mixed[1:number_of // 2 * 2:2]
    slack = jnp.minimum(lengths[donor] - 1, limit - lengths[sink]) // 2
    slack = jnp.where((donor == sequence[0]) | (sink == sequence[0]) | (lengths[sink] == 0), 0, jnp.maximum(slack, 0))
    moved = jax.random.randint(jax.random.fold_in(own, 4), (number_of // 2,), 0, 1 << 20) % (slack + 1)
    lengths = lengths.at[donor].add(-moved).at[sink].add(moved)
    items = jnp.searchsorted(jnp.cumsum(lengths), jnp.arange(rows * top), side="right").astype(jnp.int32)
    table = items.reshape(top, rows).T
    table = table[jax.random.permutation(jax.random.fold_in(own, 1), rows)]
    rotation = jax.random.randint(jax.random.fold_in(own, 2), (rows, 1), 0, top)
    return jnp.take_along_axis(table, (jnp.arange(top)[None, :] + rotation) % top, axis=1)


def portions_of(count, total, most, skew, full):
    portions = [(1 << 20) // math.isqrt(rank ** skew) + 1 for rank in range(1, count + 1)]
    largest = most if full else min(most, max(-(-total // count), total * portions[0] // sum(portions)))
    least = 1 if total - largest >= count - 1 else 0
    holding, rest = [largest] + [least] * (count - 1), total - largest - least * (count - 1)
    while rest > 0:
        free = [i for i in range(1, count) if holding[i] < largest] or [i for i in range(1, count) if holding[i] < most]
        pool, remaining = sum([portions[i] for i in free]), rest
        for i in free:
            extra = min(most - holding[i], max(1, remaining * portions[i] // pool), rest)
            holding[i] = holding[i] + extra
            rest = rest - extra
    return np.array(holding)


def normal_values(rng, shape, scale, limit, split=(), held_as=jnp.bfloat16):
    factor_of = block_levels(rng, shape, split, -0.22, 0.18) if split else 1.0
    result = jax.random.normal(rng, shape, jnp.float32) * scale * factor_of
    return jnp.minimum(jnp.maximum(result, -limit), limit).astype(held_as)


def setup_inputs(seed: int = 0, part: int = 0) -> dict:
    splits = jax.random.split(jax.random.key(seed), 6)
    part_keys = jax.random.split(jax.random.fold_in(splits[5], part), 6)
    enc_rows = normal_values(part_keys[0], (SAMPLES, H), 1.0, 6.0, ((0, 8), (1, 2)))
    shortlist_keys = jax.random.split(jax.random.fold_in(part_keys[1], 1), SAMPLES // S_DEV)
    shortlist_turns = jax.random.permutation(jax.random.fold_in(part_keys[1], 3), SAMPLES // S_DEV)
    shortlist = jax.vmap(lambda own, number: assign_block(jax.random.fold_in(part_keys[1], 2), own, number, S_DEV, CLUSTERS, K, MOST, 2))(shortlist_keys, shortlist_turns).reshape((SAMPLES, K))
    cluster_slot = jax.random.permutation(splits[2], CLUSTERS).astype(jnp.int32)
    positives = place_ends(jax.random.randint(part_keys[3], (SAMPLES, P_SIZE), 0, K * B), jax.random.fold_in(part_keys[3], 1), 0, (K * B) - 1).astype(jnp.int32)
    panels = normal_values(splits[4], (CLUSTERS, H, B), H ** -0.5, 0.125, ((0, 4), (1, 2)))
    return dict(enc_rows=enc_rows, shortlist=shortlist, cluster_slot=cluster_slot, positives=positives, panels=panels)


def reference(enc_rows, shortlist, cluster_slot, positives, panels):
    shards = SAMPLES // S_DEV
    pair_total = SAMPLES * K
    slot = jnp.take(cluster_slot, shortlist, axis=0).astype(jnp.int32)
    flat_slot = slot.reshape(shards, S_DEV * K)
    cluster_ids = jnp.arange(CLUSTERS, dtype=jnp.int32)
    placed = (flat_slot[:, :, None] == cluster_ids[None, None, :]).astype(jnp.int32)
    ranking = jnp.sum((jnp.cumsum(placed, axis=1) - 1) * placed, axis=2)
    place = jnp.arange(shards, dtype=jnp.int32)[:, None] * MOST + ranking
    table = jnp.full((CLUSTERS, shards * MOST), -1, jnp.int32)
    table = table.at[flat_slot.reshape(-1), place.reshape(-1)].set(jnp.arange(pair_total, dtype=jnp.int32))
    label_ids = jnp.arange(B, dtype=jnp.int32)

    def per_cluster(total, inputs):
        entries, weight = inputs
        present = entries >= 0
        source = jnp.maximum(entries, 0)
        sample = (source // K).astype(jnp.int32)
        beam_pos = (source % K).astype(jnp.int32)
        picked = jnp.take(enc_rows, sample, axis=0)
        picked = jnp.where(present[:, None], picked, jnp.zeros((), enc_rows.dtype))
        logits = jnp.dot(picked, weight, preferred_element_type=jnp.float32)
        wanted = jnp.take(positives, sample, axis=0) - (beam_pos * B)[:, None]
        target = jnp.any(wanted[:, :, None] == label_ids[None, None, :], axis=1)
        target = jnp.logical_and(target, present[:, None]).astype(jnp.float32)
        logit_grad = (jax.nn.sigmoid(logits) - target).astype(jnp.bfloat16)
        pair_grad = jnp.dot(logit_grad, weight.T, preferred_element_type=jnp.float32).astype(jnp.bfloat16)
        addend = jnp.where(present[:, None], pair_grad.astype(jnp.float32), jnp.zeros((), jnp.float32))
        total = total.at[sample].add(addend)
        panel_part = jnp.dot(picked.T, logit_grad, preferred_element_type=jnp.float32)
        return total, panel_part

    start = jnp.zeros((SAMPLES, H), jnp.float32)
    total, panel_grad = lax.scan(per_cluster, start, (table, panels))
    return total.astype(jnp.bfloat16), panel_grad
```

```python
import functools

import jax
import jax.numpy as jnp
from jax import lax
from jax.experimental import pallas as pl
from jax.experimental.pallas import tpu as pltpu
from jax.sharding import PartitionSpec as P


def label_slots(shortlist, cluster_slot, positives, label_width):
    clusters = jnp.arange(cluster_slot.shape[0], dtype=jnp.int32)
    named = (shortlist[:, :, None] == clusters).astype(jnp.int32)
    slots = jnp.sum(named * cluster_slot, axis=2)
    beams = jnp.arange(shortlist.shape[1], dtype=jnp.int32)
    picked = (positives[:, :, None] // label_width == beams).astype(jnp.int32)
    pos_slot = jnp.sum(picked * slots[:, None, :], axis=2)
    return slots, pos_slot, positives % label_width


def array_body(enc_rows, shortlist, cluster_slot, positives, panels):
    samples, half = enc_rows.shape
    own, _, width = panels.shape
    labs = lax.axis_size("lab")
    slots, pos_slot, pos_col = label_slots(shortlist, cluster_slot, positives, width)
    ids = jnp.concatenate([slots, pos_slot * width + pos_col], axis=1)
    all_ids = lax.all_gather(ids, "lab", axis=0, tiled=True)
    all_rows = lax.all_gather(enc_rows, "lab", axis=0, tiled=True)
    beam = shortlist.shape[1]
    first = lax.axis_index("lab") * own
    columns = first * width + jnp.arange(own * width, dtype=jnp.int32)
    present = jnp.any(all_ids[:, :beam, None] == columns[None, None, :] // width, axis=1)
    target = jnp.any(all_ids[:, beam:, None] == columns[None, None, :], axis=1)
    flat = panels.transpose(1, 0, 2).reshape(half, own * width)
    partial = jnp.dot(all_rows, flat, preferred_element_type=jnp.float32)
    logits = lax.psum(partial, "sub")
    grad = jnp.where(present, jax.nn.sigmoid(logits) - target.astype(jnp.float32), 0.0)
    grad = grad.astype(jnp.bfloat16)
    back = lax.dot_general(
        grad, flat, (((1,), (1,)), ((), ())), preferred_element_type=jnp.float32
    ).astype(jnp.bfloat16)
    returned = lax.all_to_all(
        back.reshape(labs, samples, half), "lab", split_axis=0, concat_axis=0, tiled=True
    )
    enc_grad = jnp.sum(returned, axis=0, dtype=jnp.float32).astype(jnp.bfloat16)
    part = jnp.einsum(
        "rh,rcb->chb",
        all_rows,
        grad.reshape(labs * samples, own, width),
        preferred_element_type=jnp.float32,
    )
    panel_grad = lax.psum_scatter(part, "dp", scatter_dimension=0, tiled=True)
    return enc_grad, panel_grad


CUTS = 2
MESH = pl.DeviceIdType.MESH


def pick(u, values):
    out = jnp.int32(values[-1])
    for i in range(len(values) - 2, -1, -1):
        out = jnp.where(u == i, values[i], out)
    return out


def unit_of(u, edge):
    off = jnp.where(edge, pick(u, (0, 0, 1, 2, 3, 3, 2, 1)), pick(u, (0, 0, -1, 1, -1, 2, 2, 1)))
    cut = jnp.where(edge, pick(u, (0, 1, 0, 0, 0, 1, 1, 1)), pick(u, (0, 1, 0, 0, 1, 0, 1, 1)))
    return off, cut


def step_kernel(
    dims, short_ref, pos_ref, slot_ref, enc_ref, panel_ref, enc_out, panel_out,
    rows, rows_t, ids_buf, pan, pan_t, part, other, want, grads, held, sent, got,
    twin_t, twin_g, share_out, share_in,
    load_sem, row_send, row_recv, id_send, id_recv, lx_send, lx_recv, rt_send, rt_recv,
    tt_send, tt_recv, tg_send, tg_recv, fw_send, fw_recv, sh_send, sh_recv,
):
    labs, dps, own, beam, picks, width, clusters = dims
    half, size = rows_t.shape[2], rows_t.shape[3]
    cols = own * width
    keep = own // dps
    split = twin_t.shape[2]
    me = lax.axis_index("lab")
    dp = lax.axis_index("dp")
    core = lax.axis_index("sub")
    edge = (me == 0) | (me == labs - 1)
    mid = jnp.logical_not(edge)
    low = me < labs // 2
    step = jnp.where(low, 1, -1)
    away = jnp.where(low, 1, 0)
    home = 1 - away
    units = [(b, q) for b in range(labs) for q in range(CUTS)]

    loads = [
        pltpu.make_async_copy(enc_ref.at[q], rows.at[me, q], load_sem.at[q]) for q in range(CUTS)
    ] + [
        pltpu.make_async_copy(panel_ref.at[c], pan.at[c], load_sem.at[CUTS + c]) for c in range(own)
    ]
    for load in loads:
        load.start()

    barrier = pltpu.get_barrier_semaphore()
    for off in range(1, labs):
        pl.semaphore_signal(barrier, inc=1, device_id={"lab": (me + off) % labs}, device_id_type=MESH)
    pl.semaphore_signal(barrier, inc=1, device_id={"dp": 1 - dp}, device_id_type=MESH)
    pl.semaphore_signal(barrier, inc=1, device_id={"sub": 1 - core}, device_id_type=MESH)

    short = short_ref[...]
    slots = jnp.zeros(short.shape, jnp.int32)
    for c in range(clusters):
        slots = jnp.where(short == c, slot_ref[c], slots)
    pos = pos_ref[...]
    spot = jnp.zeros(pos.shape, jnp.int32)
    for k in range(beam):
        local = pos - k * width
        spot = jnp.where((local >= 0) & (local < width), slots[k:k + 1] * width + local, spot)
    for q in range(CUTS):
        ids_buf[me, q] = spot[:, q * size:(q + 1) * size].astype(jnp.int16)
    ids_buf[me, CUTS] = jnp.concatenate(
        [slots[:, q * size:(q + 1) * size] for q in range(CUTS)], axis=0
    ).astype(jnp.int16)

    def remote(src, dst, send, recv, where):
        return pltpu.make_async_remote_copy(
            src_ref=src, dst_ref=dst, send_sem=send, recv_sem=recv,
            device_id=where, device_id_type=MESH,
        )

    def beside(side):
        return {"lab": jnp.clip(me + 2 * side - 1, 0, labs - 1)}

    def row_copy(block, cut, side):
        return remote(
            rows.at[block, cut], rows.at[block, cut],
            row_send.at[side, block, cut], row_recv.at[block, cut], beside(side),
        )

    def id_copy(off):
        return remote(
            ids_buf.at[me], ids_buf.at[me], id_send.at[off], id_recv.at[me], {"lab": (me + off) % labs}
        )

    def id_arrival(block):
        return remote(
            ids_buf.at[block], ids_buf.at[block], id_send.at[0], id_recv.at[block], beside(0)
        )

    def lx_copy(block, cut):
        return remote(
            part.at[block, cut], other.at[block, cut],
            lx_send.at[block, cut], lx_recv.at[block, cut], {"sub": 1 - core},
        )

    def back_copy(block, cut, side):
        return remote(
            sent.at[block, cut], got.at[side, block, cut],
            rt_send.at[block, cut], rt_recv.at[side, block, cut], beside(side),
        )

    def twin_rows(block, cut):
        return remote(
            rows_t.at[block, cut, pl.ds(0, split)], twin_t.at[block, cut],
            tt_send.at[block, cut], tt_recv.at[block, cut], {"dp": 1 - dp},
        )

    def twin_grads(block, cut):
        return remote(
            grads.at[block, cut, (1 - dp) * keep + core], twin_g.at[core, block, cut],
            tg_send.at[block, cut], tg_recv.at[block, cut], {"dp": 1 - dp},
        )

    def hand_over(j, block, cut):
        return remote(
            twin_g.at[j, block, cut], twin_g.at[j, block, cut],
            fw_send.at[block, cut], fw_recv.at[block, cut], {"sub": 1 - core},
        )

    def share_copy(j):
        return remote(
            share_out.at[j], share_in.at[j], sh_send.at[j], sh_recv.at[j], {"dp": 1 - dp}
        )

    pl.semaphore_wait(barrier, labs + 1)

    for off in range(1, labs):
        id_copy(off).start()
    for q in range(CUTS):
        loads[q].wait()
    row_copy(me, 0, away).start()

    @pl.when(edge)
    def _():
        row_copy(me, 1, away).start()

    @pl.when(mid)
    def _():
        row_copy(me, 0, home).start()

    lane = lax.broadcasted_iota(jnp.int32, (1, width), 1).astype(jnp.float32)
    for c in range(own):
        loads[CUTS + c].wait()

    def take(u):
        off, cut = unit_of(u, edge)
        block = me + off * step

        @pl.when(off != 0)
        def _():
            row_copy(block, cut, 0).wait_recv()

        @pl.when(mid & (off < 0))
        def _():
            row_copy(block, cut, away).start()

        @pl.when(mid & (off > 0))
        def _():
            row_copy(block, cut, home).start()

        @pl.when(mid & (off < 0) & (cut == 1))
        def _():
            row_copy(me, 1, away).start()

        @pl.when(mid & (off == 1) & (cut == 1))
        def _():
            row_copy(me, 1, home).start()

        unit = rows[block, cut]
        for c in range(own):
            part[block, cut, :, c * width:(c + 1) * width] = jnp.dot(
                unit, pan[c], preferred_element_type=jnp.float32
            )
        lx_copy(block, cut).start()
        rows_t[block, cut] = unit.T
        twin_rows(block, cut).start()

        @pl.when((off != 0) & (cut == 0))
        def _():
            id_arrival(block).wait_recv()

        spots = ids_buf[block, cut].astype(jnp.int32)
        named = ids_buf[block, CUTS].astype(jnp.int32)
        named = jnp.where(cut == 0, named[:beam], named[beam:])
        ids = jnp.concatenate([named, spots], axis=0).astype(jnp.float32)
        ids = jnp.concatenate([ids, jnp.zeros((128 - beam - picks, size), jnp.float32)], axis=0).T
        for c in range(own):
            slot = (me * own + c).astype(jnp.float32)
            present = jnp.zeros((size, 1), jnp.bool_)
            for k in range(beam):
                present = present | (ids[:, k:k + 1] == slot)
            here = lane + slot * width
            target = jnp.zeros((size, width), jnp.float32)
            for i in range(beam, beam + picks):
                target = jnp.where(ids[:, i:i + 1] == here, 1.0, target)
            want[u % 2, :, c * width:(c + 1) * width] = jnp.where(present, target, 2.0)

    def pass_on(block, cut, side):
        back_copy(block, cut, side).wait_recv()
        sent[block, cut] = (
            held[block, cut] + got[side, block, cut].astype(jnp.float32)
        ).astype(jnp.bfloat16)
        back_copy(block, cut, side).start()

    def give(u):
        off, cut = unit_of(u, edge)
        block = me + off * step

        @pl.when(mid & (u == labs * CUTS - 1))
        def _():
            pass_on(me + step, 0, away)

        lx_copy(block, cut).wait_recv()
        pieces = []
        for c in range(own):
            spread = slice(c * width, (c + 1) * width)
            logit = part[block, cut, :, spread] + other[block, cut, :, spread]
            goal = want[u % 2, :, spread]
            grad = jnp.where(goal > 1.5, 0.0, jax.nn.sigmoid(logit) - goal).astype(jnp.bfloat16)
            grads[block, cut, c] = grad
            pieces.append(grad)
        twin_grads(block, cut).start()
        total = jnp.dot(
            jnp.concatenate(pieces, axis=1), pan_t[...], preferred_element_type=jnp.float32
        )

        @pl.when(mid | (off == 0))
        def _():
            held[block, cut] = total

        @pl.when(edge & (off > 0))
        def _():
            sent[block, cut] = total.astype(jnp.bfloat16)
            back_copy(block, cut, away).start()

    @pl.loop(0, 2 * labs * CUTS)
    def _(t):
        paired = (t < 4) | (mid & (t < 12))
        turn = t % 4
        kind = jnp.where(paired, turn // 2, turn % 2)
        u = 2 * (t // 4) + jnp.where(paired, turn % 2, turn // 2)

        @pl.when(kind == 0)
        def _():
            take(u)

        @pl.when(t == 1)
        def _():
            for c in range(own):
                pan_t[c * width:(c + 1) * width, :] = pan[c].T

        @pl.when(kind == 1)
        def _():
            give(u)

    def tall(c):
        return jnp.concatenate([grads[b, q, c] for b, q in units], axis=0)

    for j in range(keep):
        late = jnp.concatenate([rows_t[b, q, split:] for b, q in units], axis=1)
        share_out[j] = jnp.dot(
            late, tall((1 - dp) * keep + j), preferred_element_type=jnp.float32
        ).astype(jnp.bfloat16)
        share_copy(j).start()

        @pl.when(mid & (j == 0))
        def _():
            pass_on(me + 2 * step, 0, away)

    @pl.when(mid)
    def _():
        pass_on(me - step, 0, home)
        pass_on(me + 2 * step, 1, away)

    @pl.loop(0, labs * CUTS)
    def _(u):
        off, cut = unit_of(u, edge)
        block = me + off * step
        twin_grads(block, cut).wait_recv()
        hand_over(core, block, cut).start()

    for j in range(keep):
        panel_out[j, split:] = jnp.dot(
            jnp.concatenate([rows_t[b, q, split:] for b, q in units], axis=1),
            tall(dp * keep + j), preferred_element_type=jnp.float32,
        )
        panel_out[j, :split] = jnp.dot(
            jnp.concatenate([rows_t[b, q, :split] for b, q in units], axis=1),
            tall(dp * keep + j), preferred_element_type=jnp.float32,
        )

    @pl.when(mid)
    def _():
        pass_on(me - step, 1, home)
        pass_on(me + step, 1, away)

    for b, q in units:
        twin_rows(b, q).wait_recv()
        hand_over(1 - core, b, q).wait_recv()
    for j in range(keep):
        panel_out[j, :split] += jnp.dot(
            jnp.concatenate([twin_t[b, q] for b, q in units], axis=1),
            jnp.concatenate([twin_g[j, b, q] for b, q in units], axis=0),
            preferred_element_type=jnp.float32,
        )

    for q in range(CUTS):
        @pl.when(mid)
        def _():
            back_copy(me, q, away).wait_recv()
            held[me, q] += got[away, me, q].astype(jnp.float32)

        back_copy(me, q, home).wait_recv()
        enc_out[q] = (held[me, q] + got[home, me, q].astype(jnp.float32)).astype(jnp.bfloat16)

    for j in range(keep):
        share_copy(j).wait_recv()
        panel_out[j, split:] += share_in[j].astype(jnp.float32)

    for off in range(1, labs):
        id_copy(off).wait_send()
    for j in range(keep):
        share_copy(j).wait_send()
    for block, cut in units:
        lx_copy(block, cut).wait_send()
        twin_rows(block, cut).wait_send()
        twin_grads(block, cut).wait_send()
        hand_over(core, block, cut).wait_send()
        off = (block - me) * step

        @pl.when((off == 0) | (mid & (off < 0)))
        def _():
            row_copy(block, cut, away).wait_send()

        @pl.when(mid & (off >= 0))
        def _():
            row_copy(block, cut, home).wait_send()

        @pl.when(off != 0)
        def _():
            back_copy(block, cut, 0).wait_send()


def kernel_body(enc_rows, shortlist, cluster_slot, positives, panels):
    samples, half = enc_rows.shape
    own, _, width = panels.shape
    labs, dps = lax.axis_size("lab"), lax.axis_size("dp")
    beam, picks = shortlist.shape[1], positives.shape[1]
    size = samples // CUTS
    keep = own // dps
    split = half // 2
    f32, bf16 = jnp.float32, jnp.bfloat16
    vmem, dma = pltpu.VMEM, pltpu.SemaphoreType.DMA
    whole = pl.BlockSpec(memory_space=pltpu.VMEM)
    there = pl.BlockSpec(memory_space=pl.ANY)
    enc_grad, panel_grad = pl.pallas_call(
        functools.partial(
            step_kernel, (labs, dps, own, beam, picks, width, cluster_slot.shape[0])
        ),
        out_shape=(
            jax.ShapeDtypeStruct((CUTS, size, half), bf16),
            jax.ShapeDtypeStruct((keep, half, width), f32),
        ),
        in_specs=[whole, whole, pl.BlockSpec(memory_space=pltpu.SMEM), there, there],
        out_specs=(whole, whole),
        scratch_shapes=[
            vmem((labs, CUTS, size, half), bf16),
            vmem((labs, CUTS, half, size), bf16),
            vmem((labs, CUTS + 1, picks, size), jnp.int16),
            vmem((own, half, width), bf16),
            vmem((own * width, half), bf16),
            vmem((labs, CUTS, size, own * width), f32),
            vmem((labs, CUTS, size, own * width), f32),
            vmem((2, size, own * width), f32),
            vmem((labs, CUTS, own, size, width), bf16),
            vmem((labs, CUTS, size, half), f32),
            vmem((labs, CUTS, size, half), bf16),
            vmem((2, labs, CUTS, size, half), bf16),
            vmem((labs, CUTS, split, size), bf16),
            vmem((keep, labs, CUTS, size, width), bf16),
            vmem((keep, half - split, width), bf16),
            vmem((keep, half - split, width), bf16),
            dma((CUTS + own,)),
            dma((2, labs, CUTS)),
            dma((labs, CUTS)),
            dma((labs,)),
            dma((labs,)),
            dma((labs, CUTS)),
            dma((labs, CUTS)),
            dma((labs, CUTS)),
            dma((2, labs, CUTS)),
            dma((labs, CUTS)),
            dma((labs, CUTS)),
            dma((labs, CUTS)),
            dma((labs, CUTS)),
            dma((labs, CUTS)),
            dma((labs, CUTS)),
            dma((keep,)),
            dma((keep,)),
        ],
        compiler_params=pltpu.CompilerParams(
            collective_id=0, has_side_effects=True, vmem_limit_bytes=56 << 20
        ),
    )(shortlist.T, positives.T, cluster_slot, enc_rows.reshape(CUTS, size, half), panels)
    return enc_grad.reshape(samples, half), panel_grad


def kernel_fits(enc_rows, shortlist, positives, panels):
    samples, half = enc_rows.shape
    own, _, width = panels.shape
    return (
        lax.axis_size("lab") == 4
        and lax.axis_size("dp") == 2
        and lax.axis_size("sub") == 2
        and own == 4
        and samples == CUTS * 128
        and half <= 1024
        and half % 256 == 0
        and width == 256
        and shortlist.shape[1] == 8
        and positives.shape[1] == 16
    )


def body(enc_rows, shortlist, cluster_slot, positives, panels):
    if kernel_fits(enc_rows, shortlist, positives, panels):
        return kernel_body(enc_rows, shortlist, cluster_slot, positives, panels)
    return array_body(enc_rows, shortlist, cluster_slot, positives, panels)


def solution(mesh):
    in_specs = (
        P(("grp", "lab", "dp"), "sub"),
        P(("grp", "lab", "dp"), None),
        P(),
        P(("grp", "lab", "dp"), None),
        P("lab", "sub", None),
    )
    out_specs = (P(("grp", "lab", "dp"), "sub"), P(("grp", "lab", "dp"), "sub", None))
    return jax.shard_map(body, mesh=mesh, in_specs=in_specs, out_specs=out_specs, check_vma=False)
```

```python
import functools

import jax
import jax.numpy as jnp
from jax import lax
from jax.experimental import pallas as pl
from jax.experimental.pallas import tpu as pltpu
from jax.sharding import PartitionSpec as P


def label_slots(shortlist, cluster_slot, positives, label_width):
    clusters = jnp.arange(cluster_slot.shape[0], dtype=jnp.int32)
    named = (shortlist[:, :, None] == clusters).astype(jnp.int32)
    slots = jnp.sum(named * cluster_slot, axis=2)
    beams = jnp.arange(shortlist.shape[1], dtype=jnp.int32)
    picked = (positives[:, :, None] // label_width == beams).astype(jnp.int32)
    pos_slot = jnp.sum(picked * slots[:, None, :], axis=2)
    return slots, pos_slot, positives % label_width


def array_body(enc_rows, shortlist, cluster_slot, positives, panels):
    samples, half = enc_rows.shape
    own, _, width = panels.shape
    labs = lax.axis_size("lab")
    slots, pos_slot, pos_col = label_slots(shortlist, cluster_slot, positives, width)
    ids = jnp.concatenate([slots, pos_slot * width + pos_col], axis=1)
    all_ids = lax.all_gather(ids, "lab", axis=0, tiled=True)
    all_rows = lax.all_gather(enc_rows, "lab", axis=0, tiled=True)
    beam = shortlist.shape[1]
    first = lax.axis_index("lab") * own
    columns = first * width + jnp.arange(own * width, dtype=jnp.int32)
    present = jnp.any(all_ids[:, :beam, None] == columns[None, None, :] // width, axis=1)
    target = jnp.any(all_ids[:, beam:, None] == columns[None, None, :], axis=1)
    flat = panels.transpose(1, 0, 2).reshape(half, own * width)
    partial = jnp.dot(all_rows, flat, preferred_element_type=jnp.float32)
    logits = lax.psum(partial, "sub")
    grad = jnp.where(present, jax.nn.sigmoid(logits) - target.astype(jnp.float32), 0.0)
    grad = grad.astype(jnp.bfloat16)
    back = lax.dot_general(
        grad, flat, (((1,), (1,)), ((), ())), preferred_element_type=jnp.float32
    ).astype(jnp.bfloat16)
    returned = lax.all_to_all(
        back.reshape(labs, samples, half), "lab", split_axis=0, concat_axis=0, tiled=True
    )
    enc_grad = jnp.sum(returned, axis=0, dtype=jnp.float32).astype(jnp.bfloat16)
    part = jnp.einsum(
        "rh,rcb->chb",
        all_rows,
        grad.reshape(labs * samples, own, width),
        preferred_element_type=jnp.float32,
    )
    panel_grad = lax.psum_scatter(part, "dp", scatter_dimension=0, tiled=True)
    return enc_grad, panel_grad


CUTS = 2
MESH = pl.DeviceIdType.MESH


def pick(u, values):
    out = jnp.int32(values[-1])
    for i in range(len(values) - 2, -1, -1):
        out = jnp.where(u == i, values[i], out)
    return out


def unit_of(u, edge):
    off = jnp.where(edge, pick(u, (0, 0, 1, 2, 3, 3, 2, 1)), pick(u, (0, 0, -1, 1, -1, 2, 2, 1)))
    cut = jnp.where(edge, pick(u, (0, 1, 0, 0, 0, 1, 1, 1)), pick(u, (0, 1, 0, 0, 1, 0, 1, 1)))
    return off, cut


def step_kernel(
    dims, short_ref, pos_ref, slot_ref, enc_ref, panel_ref, enc_out, panel_out,
    rows, rows_t, ids_buf, pan, pan_t, part, other, want, grads, held, sent, got,
    twin_t, twin_g, share_out, share_in,
    load_sem, row_send, row_recv, id_send, id_recv, lx_send, lx_recv, rt_send, rt_recv,
    tt_send, tt_recv, tg_send, tg_recv, fw_send, fw_recv, sh_send, sh_recv,
):
    labs, dps, own, beam, picks, width, clusters = dims
    half, size = rows_t.shape[2], rows_t.shape[3]
    cols = own * width
    keep = own // dps
    split = twin_t.shape[2]
    me = lax.axis_index("lab")
    dp = lax.axis_index("dp")
    core = lax.axis_index("sub")
    edge = (me == 0) | (me == labs - 1)
    mid = jnp.logical_not(edge)
    low = me < labs // 2
    step = jnp.where(low, 1, -1)
    away = jnp.where(low, 1, 0)
    home = 1 - away
    units = [(b, q) for b in range(labs) for q in range(CUTS)]

    loads = [
        pltpu.make_async_copy(enc_ref.at[q], rows.at[me, q], load_sem.at[q]) for q in range(CUTS)
    ] + [
        pltpu.make_async_copy(panel_ref.at[c], pan.at[c], load_sem.at[CUTS + c]) for c in range(own)
    ]
    for load in loads:
        load.start()

    barrier = pltpu.get_barrier_semaphore()
    for off in range(1, labs):
        pl.semaphore_signal(barrier, inc=1, device_id={"lab": (me + off) % labs}, device_id_type=MESH)
    pl.semaphore_signal(barrier, inc=1, device_id={"dp": 1 - dp}, device_id_type=MESH)
    pl.semaphore_signal(barrier, inc=1, device_id={"sub": 1 - core}, device_id_type=MESH)

    short = short_ref[...]
    slots = jnp.zeros(short.shape, jnp.int32)
    for c in range(clusters):
        slots = jnp.where(short == c, slot_ref[c], slots)
    pos = pos_ref[...]
    spot = jnp.zeros(pos.shape, jnp.int32)
    for k in range(beam):
        local = pos - k * width
        spot = jnp.where((local >= 0) & (local < width), slots[k:k + 1] * width + local, spot)
    for q in range(CUTS):
        ids_buf[me, q] = spot[:, q * size:(q + 1) * size].astype(jnp.int16)
    ids_buf[me, CUTS] = jnp.concatenate(
        [slots[:, q * size:(q + 1) * size] for q in range(CUTS)], axis=0
    ).astype(jnp.int16)

    def remote(src, dst, send, recv, where):
        return pltpu.make_async_remote_copy(
            src_ref=src, dst_ref=dst, send_sem=send, recv_sem=recv,
            device_id=where, device_id_type=MESH,
        )

    def beside(side):
        return {"lab": jnp.clip(me + 2 * side - 1, 0, labs - 1)}

    def row_copy(block, cut, side):
        return remote(
            rows.at[block, cut], rows.at[block, cut],
            row_send.at[side, block, cut], row_recv.at[block, cut], beside(side),
        )

    def id_copy(off):
        return remote(
            ids_buf.at[me], ids_buf.at[me], id_send.at[off], id_recv.at[me], {"lab": (me + off) % labs}
        )

    def id_arrival(block):
        return remote(
            ids_buf.at[block], ids_buf.at[block], id_send.at[0], id_recv.at[block], beside(0)
        )

    def lx_copy(block, cut):
        return remote(
            part.at[block, cut], other.at[block, cut],
            lx_send.at[block, cut], lx_recv.at[block, cut], {"sub": 1 - core},
        )

    def back_copy(block, cut, side):
        return remote(
            sent.at[block, cut], got.at[side, block, cut],
            rt_send.at[block, cut], rt_recv.at[side, block, cut], beside(side),
        )

    def twin_rows(block, cut):
        return remote(
            rows_t.at[block, cut, pl.ds(0, split)], twin_t.at[block, cut],
            tt_send.at[block, cut], tt_recv.at[block, cut], {"dp": 1 - dp},
        )

    def twin_grads(block, cut):
        return remote(
            grads.at[block, cut, (1 - dp) * keep + core], twin_g.at[core, block, cut],
            tg_send.at[block, cut], tg_recv.at[block, cut], {"dp": 1 - dp},
        )

    def hand_over(j, block, cut):
        return remote(
            twin_g.at[j, block, cut], twin_g.at[j, block, cut],
            fw_send.at[block, cut], fw_recv.at[block, cut], {"sub": 1 - core},
        )

    def share_copy(j):
        return remote(
            share_out.at[j], share_in.at[j], sh_send.at[j], sh_recv.at[j], {"dp": 1 - dp}
        )

    pl.semaphore_wait(barrier, labs + 1)

    for off in range(1, labs):
        id_copy(off).start()
    for q in range(CUTS):
        loads[q].wait()
    row_copy(me, 0, away).start()

    @pl.when(edge)
    def _():
        row_copy(me, 1, away).start()

    @pl.when(mid)
    def _():
        row_copy(me, 0, home).start()

    lane = lax.broadcasted_iota(jnp.int32, (1, width), 1).astype(jnp.float32)
    for c in range(own):
        loads[CUTS + c].wait()

    def take(u):
        off, cut = unit_of(u, edge)
        block = me + off * step

        @pl.when(off != 0)
        def _():
            row_copy(block, cut, 0).wait_recv()

        @pl.when(mid & (off < 0))
        def _():
            row_copy(block, cut, away).start()

        @pl.when(mid & (off > 0))
        def _():
            row_copy(block, cut, home).start()

        @pl.when(mid & (off < 0) & (cut == 1))
        def _():
            row_copy(me, 1, away).start()

        @pl.when(mid & (off == 1) & (cut == 1))
        def _():
            row_copy(me, 1, home).start()

        unit = rows[block, cut]
        for c in range(own):
            part[block, cut, :, c * width:(c + 1) * width] = jnp.dot(
                unit, pan[c], preferred_element_type=jnp.float32
            )
        lx_copy(block, cut).start()
        rows_t[block, cut] = unit.T
        twin_rows(block, cut).start()

        @pl.when((off != 0) & (cut == 0))
        def _():
            id_arrival(block).wait_recv()

        spots = ids_buf[block, cut].astype(jnp.int32)
        named = ids_buf[block, CUTS].astype(jnp.int32)
        named = jnp.where(cut == 0, named[:beam], named[beam:])
        ids = jnp.concatenate([named, spots], axis=0).astype(jnp.float32)
        ids = jnp.concatenate([ids, jnp.zeros((128 - beam - picks, size), jnp.float32)], axis=0).T
        for c in range(own):
            slot = (me * own + c).astype(jnp.float32)
            present = jnp.zeros((size, 1), jnp.bool_)
            for k in range(beam):
                present = present | (ids[:, k:k + 1] == slot)
            here = lane + slot * width
            target = jnp.zeros((size, width), jnp.float32)
            for i in range(beam, beam + picks):
                target = jnp.where(ids[:, i:i + 1] == here, 1.0, target)
            want[u % 2, :, c * width:(c + 1) * width] = jnp.where(present, target, 2.0)

    def pass_on(block, cut, side):
        back_copy(block, cut, side).wait_recv()
        sent[block, cut] = (
            held[block, cut] + got[side, block, cut].astype(jnp.float32)
        ).astype(jnp.bfloat16)
        back_copy(block, cut, side).start()

    def give(u):
        off, cut = unit_of(u, edge)
        block = me + off * step

        @pl.when(mid & (u == labs * CUTS - 1))
        def _():
            pass_on(me + step, 0, away)

        lx_copy(block, cut).wait_recv()
        pieces = []
        for c in range(own):
            spread = slice(c * width, (c + 1) * width)
            logit = part[block, cut, :, spread] + other[block, cut, :, spread]
            goal = want[u % 2, :, spread]
            grad = jnp.where(goal > 1.5, 0.0, jax.nn.sigmoid(logit) - goal).astype(jnp.bfloat16)
            grads[block, cut, c] = grad
            pieces.append(grad)
        twin_grads(block, cut).start()
        total = jnp.dot(
            jnp.concatenate(pieces, axis=1), pan_t[...], preferred_element_type=jnp.float32
        )

        @pl.when(mid | (off == 0))
        def _():
            held[block, cut] = total

        @pl.when(edge & (off > 0))
        def _():
            sent[block, cut] = total.astype(jnp.bfloat16)
            back_copy(block, cut, away).start()

    @pl.loop(0, 2 * labs * CUTS)
    def _(t):
        paired = (t < 4) | (mid & (t < 12))
        turn = t % 4
        kind = jnp.where(paired, turn // 2, turn % 2)
        u = 2 * (t // 4) + jnp.where(paired, turn % 2, turn // 2)

        @pl.when(kind == 0)
        def _():
            take(u)

        @pl.when(t == 1)
        def _():
            for c in range(own):
                pan_t[c * width:(c + 1) * width, :] = pan[c].T

        @pl.when(kind == 1)
        def _():
            give(u)

    def tall(c):
        return jnp.concatenate([grads[b, q, c] for b, q in units], axis=0)

    for j in range(keep):
        late = jnp.concatenate([rows_t[b, q, split:] for b, q in units], axis=1)
        share_out[j] = jnp.dot(
            late, tall((1 - dp) * keep + j), preferred_element_type=jnp.float32
        ).astype(jnp.bfloat16)
        share_copy(j).start()

        @pl.when(mid & (j == 0))
        def _():
            pass_on(me + 2 * step, 0, away)

    @pl.when(mid)
    def _():
        pass_on(me - step, 0, home)
        pass_on(me + 2 * step, 1, away)

    @pl.loop(0, labs * CUTS)
    def _(u):
        off, cut = unit_of(u, edge)
        block = me + off * step
        twin_grads(block, cut).wait_recv()
        hand_over(core, block, cut).start()

    for j in range(keep):
        panel_out[j, split:] = jnp.dot(
            jnp.concatenate([rows_t[b, q, split:] for b, q in units], axis=1),
            tall(dp * keep + j), preferred_element_type=jnp.float32,
        )
        panel_out[j, :split] = jnp.dot(
            jnp.concatenate([rows_t[b, q, :split] for b, q in units], axis=1),
            tall(dp * keep + j), preferred_element_type=jnp.float32,
        )

    @pl.when(mid)
    def _():
        pass_on(me - step, 1, home)
        pass_on(me + step, 1, away)

    for b, q in units:
        twin_rows(b, q).wait_recv()
        hand_over(1 - core, b, q).wait_recv()
    for j in range(keep):
        panel_out[j, :split] += jnp.dot(
            jnp.concatenate([twin_t[b, q] for b, q in units], axis=1),
            jnp.concatenate([twin_g[j, b, q] for b, q in units], axis=0),
            preferred_element_type=jnp.float32,
        )

    for q in range(CUTS):
        @pl.when(mid)
        def _():
            back_copy(me, q, away).wait_recv()
            held[me, q] += got[away, me, q].astype(jnp.float32)

        back_copy(me, q, home).wait_recv()
        enc_out[q] = (held[me, q] + got[home, me, q].astype(jnp.float32)).astype(jnp.bfloat16)

    for j in range(keep):
        share_copy(j).wait_recv()
        panel_out[j, split:] += share_in[j].astype(jnp.float32)

    for off in range(1, labs):
        id_copy(off).wait_send()
    for j in range(keep):
        share_copy(j).wait_send()
    for block, cut in units:
        lx_copy(block, cut).wait_send()
        twin_rows(block, cut).wait_send()
        twin_grads(block, cut).wait_send()
        hand_over(core, block, cut).wait_send()
        off = (block - me) * step

        @pl.when((off == 0) | (mid & (off < 0)))
        def _():
            row_copy(block, cut, away).wait_send()

        @pl.when(mid & (off >= 0))
        def _():
            row_copy(block, cut, home).wait_send()

        @pl.when(off != 0)
        def _():
            back_copy(block, cut, 0).wait_send()


def kernel_body(enc_rows, shortlist, cluster_slot, positives, panels):
    samples, half = enc_rows.shape
    own, _, width = panels.shape
    labs, dps = lax.axis_size("lab"), lax.axis_size("dp")
    beam, picks = shortlist.shape[1], positives.shape[1]
    size = samples // CUTS
    keep = own // dps
    split = half // 2
    f32, bf16 = jnp.float32, jnp.bfloat16
    vmem, dma = pltpu.VMEM, pltpu.SemaphoreType.DMA
    whole = pl.BlockSpec(memory_space=pltpu.VMEM)
    there = pl.BlockSpec(memory_space=pl.ANY)
    enc_grad, panel_grad = pl.pallas_call(
        functools.partial(
            step_kernel, (labs, dps, own, beam, picks, width, cluster_slot.shape[0])
        ),
        out_shape=(
            pltpu.VMEM((CUTS, size, half), bf16),
            pltpu.VMEM((keep, half, width), f32),
        ),
        in_specs=[whole, whole, pl.BlockSpec(memory_space=pltpu.SMEM), there, there],
        out_specs=(whole, whole),
        scratch_shapes=[
            vmem((labs, CUTS, size, half), bf16),
            vmem((labs, CUTS, half, size), bf16),
            vmem((labs, CUTS + 1, picks, size), jnp.int16),
            vmem((own, half, width), bf16),
            vmem((own * width, half), bf16),
            vmem((labs, CUTS, size, own * width), f32),
            vmem((labs, CUTS, size, own * width), f32),
            vmem((2, size, own * width), f32),
            vmem((labs, CUTS, own, size, width), bf16),
            vmem((labs, CUTS, size, half), f32),
            vmem((labs, CUTS, size, half), bf16),
            vmem((2, labs, CUTS, size, half), bf16),
            vmem((labs, CUTS, split, size), bf16),
            vmem((keep, labs, CUTS, size, width), bf16),
            vmem((keep, half - split, width), bf16),
            vmem((keep, half - split, width), bf16),
            dma((CUTS + own,)),
            dma((2, labs, CUTS)),
            dma((labs, CUTS)),
            dma((labs,)),
            dma((labs,)),
            dma((labs, CUTS)),
            dma((labs, CUTS)),
            dma((labs, CUTS)),
            dma((2, labs, CUTS)),
            dma((labs, CUTS)),
            dma((labs, CUTS)),
            dma((labs, CUTS)),
            dma((labs, CUTS)),
            dma((labs, CUTS)),
            dma((labs, CUTS)),
            dma((keep,)),
            dma((keep,)),
        ],
        compiler_params=pltpu.CompilerParams(
            collective_id=0, has_side_effects=True, vmem_limit_bytes=56 << 20
        ),
    )(shortlist.T, positives.T, cluster_slot, enc_rows.reshape(CUTS, size, half), panels)
    return enc_grad.reshape(samples, half), panel_grad


def kernel_fits(enc_rows, shortlist, positives, panels):
    samples, half = enc_rows.shape
    own, _, width = panels.shape
    return (
        lax.axis_size("lab") == 4
        and lax.axis_size("dp") == 2
        and lax.axis_size("sub") == 2
        and own == 4
        and samples == CUTS * 128
        and half <= 1024
        and half % 256 == 0
        and width == 256
        and shortlist.shape[1] == 8
        and positives.shape[1] == 16
    )


def body(enc_rows, shortlist, cluster_slot, positives, panels):
    if kernel_fits(enc_rows, shortlist, positives, panels):
        return kernel_body(enc_rows, shortlist, cluster_slot, positives, panels)
    return array_body(enc_rows, shortlist, cluster_slot, positives, panels)


def solution(mesh):
    in_specs = (
        P(("grp", "lab", "dp"), "sub"),
        P(("grp", "lab", "dp"), None),
        P(),
        P(("grp", "lab", "dp"), None),
        P("lab", "sub", None),
    )
    out_specs = (P(("grp", "lab", "dp"), "sub"), P(("grp", "lab", "dp"), "sub", None))
    return jax.shard_map(body, mesh=mesh, in_specs=in_specs, out_specs=out_specs, check_vma=False)
```

```python
import functools

import jax
import jax.numpy as jnp
from jax import lax
from jax.experimental import pallas as pl
from jax.experimental.pallas import tpu as pltpu
from jax.sharding import PartitionSpec as P


def label_slots(shortlist, cluster_slot, positives, label_width):
    clusters = jnp.arange(cluster_slot.shape[0], dtype=jnp.int32)
    named = (shortlist[:, :, None] == clusters).astype(jnp.int32)
    slots = jnp.sum(named * cluster_slot, axis=2)
    beams = jnp.arange(shortlist.shape[1], dtype=jnp.int32)
    picked = (positives[:, :, None] // label_width == beams).astype(jnp.int32)
    pos_slot = jnp.sum(picked * slots[:, None, :], axis=2)
    return slots, pos_slot, positives % label_width


def array_body(enc_rows, shortlist, cluster_slot, positives, panels):
    samples, half = enc_rows.shape
    own, _, width = panels.shape
    labs = lax.axis_size("lab")
    slots, pos_slot, pos_col = label_slots(shortlist, cluster_slot, positives, width)
    ids = jnp.concatenate([slots, pos_slot * width + pos_col], axis=1)
    all_ids = lax.all_gather(ids, "lab", axis=0, tiled=True)
    all_rows = lax.all_gather(enc_rows, "lab", axis=0, tiled=True)
    beam = shortlist.shape[1]
    first = lax.axis_index("lab") * own
    columns = first * width + jnp.arange(own * width, dtype=jnp.int32)
    present = jnp.any(all_ids[:, :beam, None] == columns[None, None, :] // width, axis=1)
    target = jnp.any(all_ids[:, beam:, None] == columns[None, None, :], axis=1)
    flat = panels.transpose(1, 0, 2).reshape(half, own * width)
    partial = jnp.dot(all_rows, flat, preferred_element_type=jnp.float32)
    logits = lax.psum(partial, "sub")
    grad = jnp.where(present, jax.nn.sigmoid(logits) - target.astype(jnp.float32), 0.0)
    grad = grad.astype(jnp.bfloat16)
    back = lax.dot_general(
        grad, flat, (((1,), (1,)), ((), ())), preferred_element_type=jnp.float32
    ).astype(jnp.bfloat16)
    returned = lax.all_to_all(
        back.reshape(labs, samples, half), "lab", split_axis=0, concat_axis=0, tiled=True
    )
    enc_grad = jnp.sum(returned, axis=0, dtype=jnp.float32).astype(jnp.bfloat16)
    part = jnp.einsum(
        "rh,rcb->chb",
        all_rows,
        grad.reshape(labs * samples, own, width),
        preferred_element_type=jnp.float32,
    )
    panel_grad = lax.psum_scatter(part, "dp", scatter_dimension=0, tiled=True)
    return enc_grad, panel_grad


CUTS = 2
MESH = pl.DeviceIdType.MESH


def pick(u, values):
    out = jnp.int32(values[-1])
    for i in range(len(values) - 2, -1, -1):
        out = jnp.where(u == i, values[i], out)
    return out


EDGE_TURNS = (
    (0, 0), (0, 1), (1, 0), (1, 1), (0, 2), (1, 2), (0, 3), (1, 3),
    (0, 4), (1, 4), (0, 5), (1, 5), (0, 6), (1, 6), (0, 7), (1, 7),
)
MID_TURNS = (
    (0, 0), (0, 1), (2, 0), (1, 0), (2, 1), (1, 1), (0, 2), (0, 3), (2, 2), (1, 2), (1, 3), (2, 3),
    (0, 4), (0, 5), (2, 4), (1, 4), (1, 5), (2, 5), (0, 6), (2, 6), (1, 6), (3, 0), (2, 7), (0, 7),
    (3, 1), (1, 7),
)
PARTS = 2
WIDE = 2


def unit_of(u, edge):
    off = jnp.where(edge, pick(u, (0, 0, 1, 2, 3, 3, 2, 1)), pick(u, (0, 0, -1, 1, -1, 2, 2, 1)))
    cut = jnp.where(edge, pick(u, (0, 1, 0, 0, 0, 1, 1, 1)), pick(u, (0, 1, 0, 0, 1, 0, 1, 1)))
    return off, cut


def step_kernel(
    dims, short_hbm, pos_hbm, slot_hbm, enc_ref, panel_ref, enc_out, panel_out,
    short_ref, pos_ref, slot_ref,
    rows, rows_t, ids_buf, pan, pan_t, part, other, want, grads, held, sent, got,
    twin_t, twin_g, share_out, share_in,
    load_sem, row_send, row_recv, id_send, id_recv, lx_send, lx_recv, rt_send, rt_recv,
    tt_send, tt_recv, tg_send, tg_recv, fw_send, fw_recv, sh_send, sh_recv,
):
    labs, dps, own, beam, picks, width, clusters = dims
    half, size = rows_t.shape[2], rows_t.shape[3]
    keep = own // dps
    split = twin_t.shape[2]
    piece = size // PARTS
    pieces = CUTS * PARTS
    pair = own // WIDE
    me = lax.axis_index("lab")
    dp = lax.axis_index("dp")
    core = lax.axis_index("sub")
    edge = (me == 0) | (me == labs - 1)
    mid = jnp.logical_not(edge)
    low = me < labs // 2
    step = jnp.where(low, 1, -1)
    away = jnp.where(low, 1, 0)
    home = 1 - away
    units = [(b, q) for b in range(labs) for q in range(CUTS)]

    barrier = pltpu.get_barrier_semaphore()
    for off in range(1, labs):
        pl.semaphore_signal(barrier, inc=1, device_id={"lab": (me + off) % labs}, device_id_type=MESH)
    pl.semaphore_signal(barrier, inc=1, device_id={"dp": 1 - dp}, device_id_type=MESH)
    pl.semaphore_signal(barrier, inc=1, device_id={"sub": 1 - core}, device_id_type=MESH)

    loads = [
        pltpu.make_async_copy(enc_ref.at[q], rows.at[me, q], load_sem.at[q]) for q in range(CUTS)
    ] + [
        pltpu.make_async_copy(panel_ref.at[c], pan.at[c], load_sem.at[CUTS + c]) for c in range(own)
    ]
    small = [
        pltpu.make_async_copy(short_hbm, short_ref, load_sem.at[CUTS + own]),
        pltpu.make_async_copy(pos_hbm, pos_ref, load_sem.at[CUTS + own + 1]),
        pltpu.make_async_copy(slot_hbm, slot_ref, load_sem.at[CUTS + own + 2]),
    ]
    for load in small + loads:
        load.start()

    def remote(src, dst, send, recv, where):
        return pltpu.make_async_remote_copy(
            src_ref=src, dst_ref=dst, send_sem=send, recv_sem=recv,
            device_id=where, device_id_type=MESH,
        )

    def beside(side):
        return {"lab": jnp.clip(me + 2 * side - 1, 0, labs - 1)}

    def spot_of(p):
        return p // PARTS, pl.ds(pl.multiple_of((p % PARTS) * piece, piece), piece)

    def row_copy(block, p, side, src=None):
        cut, span = spot_of(p)
        here = rows.at[block, cut, span]
        return remote(
            here if src is None else src.at[cut, span], here,
            row_send.at[side, block, p], row_recv.at[block, p], beside(side),
        )

    def id_copy(off):
        return remote(
            ids_buf.at[me], ids_buf.at[me], id_send.at[off], id_recv.at[me], {"lab": (me + off) % labs}
        )

    def id_arrival(block):
        return remote(
            ids_buf.at[block], ids_buf.at[block], id_send.at[0], id_recv.at[block], beside(0)
        )

    def lx_copy(block, cut, w):
        return remote(
            part.at[block, cut, w], other.at[block, cut, w],
            lx_send.at[block, cut, w], lx_recv.at[block, cut, w], {"sub": 1 - core},
        )

    def back_copy(block, p, side):
        cut, span = spot_of(p)
        return remote(
            sent.at[block, cut, span], got.at[side, block, cut, span],
            rt_send.at[block, p], rt_recv.at[side, block, p], beside(side),
        )

    def twin_rows(block, cut):
        return remote(
            rows_t.at[block, cut, pl.ds(0, split)], twin_t.at[block, cut],
            tt_send.at[block, cut], tt_recv.at[block, cut], {"dp": 1 - dp},
        )

    def twin_grads(block, cut):
        return remote(
            grads.at[block, cut, (1 - dp) * keep + core], twin_g.at[core, block, cut],
            tg_send.at[block, cut], tg_recv.at[block, cut], {"dp": 1 - dp},
        )

    def hand_over(j, block, cut):
        return remote(
            twin_g.at[j, block, cut], twin_g.at[j, block, cut],
            fw_send.at[block, cut], fw_recv.at[block, cut], {"sub": 1 - core},
        )

    def share_copy(j):
        return remote(
            share_out.at[j], share_in.at[j], sh_send.at[j], sh_recv.at[j], {"dp": 1 - dp}
        )

    pl.semaphore_wait(barrier, labs + 1)

    for p in range(PARTS):
        row_copy(me, p, away, enc_ref).start()

        @pl.when(mid)
        def _():
            row_copy(me, p, home, enc_ref).start()

    for load in small:
        load.wait()
    short = short_ref[...]
    slots = jnp.zeros(short.shape, jnp.int32)
    for c in range(clusters):
        slots = jnp.where(short == c, slot_ref[c], slots)
    pos = pos_ref[...]
    spot = jnp.zeros(pos.shape, jnp.int32)
    for k in range(beam):
        local = pos - k * width
        spot = jnp.where((local >= 0) & (local < width), slots[k:k + 1] * width + local, spot)
    for q in range(CUTS):
        ids_buf[me, q] = spot[:, q * size:(q + 1) * size].astype(jnp.int16)
    ids_buf[me, CUTS] = jnp.concatenate(
        [slots[:, q * size:(q + 1) * size] for q in range(CUTS)], axis=0
    ).astype(jnp.int16)
    for off in range(1, labs):
        id_copy(off).start()

    @pl.when(edge)
    def _():
        for p in range(PARTS, pieces):
            row_copy(me, p, away, enc_ref).start()

    for load in loads:
        load.wait()
    lane = lax.broadcasted_iota(jnp.int32, (1, width), 1).astype(jnp.float32)

    def forward(i):
        off = pick(i, (1, 1, 2, 2, 2, 2, 1, 1))
        p = pick(i, (0, 1, 0, 1, 2, 3, 2, 3))

        @pl.when(i < pieces)
        def _():
            row_copy(me - step, i, 0).wait_recv()
            row_copy(me - step, i, away).start()

        row_copy(me + off * step, p, 0).wait_recv()
        row_copy(me + off * step, p, home).start()

        @pl.when(i == pieces - 1)
        def _():
            for late in range(PARTS, pieces):
                row_copy(me, late, away, enc_ref).start()

        @pl.when(i == 2 * pieces - 1)
        def _():
            for late in range(PARTS, pieces):
                row_copy(me, late, home, enc_ref).start()

    def take(u):
        off, cut = unit_of(u, edge)
        block = me + off * step

        @pl.when(edge & (off != 0))
        def _():
            for i in range(PARTS):
                row_copy(block, cut * PARTS + i, 0).wait_recv()

        unit = rows[block, cut]
        for w in range(WIDE):
            for i in range(pair):
                part[block, cut, w, :, i * width:(i + 1) * width] = jnp.dot(
                    unit, pan[w * pair + i], preferred_element_type=jnp.float32
                )
            lx_copy(block, cut, w).start()
        rows_t[block, cut] = unit.T
        twin_rows(block, cut).start()

        @pl.when((off != 0) & (cut == 0))
        def _():
            id_arrival(block).wait_recv()

        spots = ids_buf[block, cut].astype(jnp.int32)
        named = ids_buf[block, CUTS].astype(jnp.int32)
        named = jnp.where(cut == 0, named[:beam], named[beam:])
        ids = jnp.concatenate([named, spots], axis=0).astype(jnp.float32)
        ids = jnp.concatenate([ids, jnp.zeros((128 - beam - picks, size), jnp.float32)], axis=0).T
        for c in range(own):
            slot = (me * own + c).astype(jnp.float32)
            present = jnp.zeros((size, 1), jnp.bool_)
            for k in range(beam):
                present = present | (ids[:, k:k + 1] == slot)
            here = lane + slot * width
            target = jnp.zeros((size, width), jnp.float32)
            for i in range(beam, beam + picks):
                target = jnp.where(ids[:, i:i + 1] == here, 1.0, target)
            want[u % 2, :, c * width:(c + 1) * width] = jnp.where(present, target, 2.0)

    def pass_on(block, p, side):
        cut, span = spot_of(p)
        back_copy(block, p, side).wait_recv()
        sent[block, cut, span] = (
            held[block, cut, span] + got[side, block, cut, span].astype(jnp.float32)
        ).astype(jnp.bfloat16)
        back_copy(block, p, side).start()

    def give(u):
        off, cut = unit_of(u, edge)
        block = me + off * step
        row = []
        for w in range(WIDE):
            lx_copy(block, cut, w).wait_recv()
            for i in range(pair):
                c = w * pair + i
                spread = slice(i * width, (i + 1) * width)
                logit = part[block, cut, w, :, spread] + other[block, cut, w, :, spread]
                goal = want[u % 2, :, c * width:(c + 1) * width]
                grad = jnp.where(goal > 1.5, 0.0, jax.nn.sigmoid(logit) - goal).astype(jnp.bfloat16)
                grads[block, cut, c] = grad
                row.append(grad)
        twin_grads(block, cut).start()
        total = jnp.dot(
            jnp.concatenate(row, axis=1), pan_t[...], preferred_element_type=jnp.float32
        )

        @pl.when(mid | (off == 0))
        def _():
            held[block, cut] = total

        @pl.when(edge & (off > 0))
        def _():
            sent[block, cut] = total.astype(jnp.bfloat16)
            for i in range(PARTS):
                back_copy(block, cut * PARTS + i, away).start()

    @pl.loop(0, jnp.where(edge, len(EDGE_TURNS), len(MID_TURNS)))
    def _(t):
        edge_turn = pick(t, tuple(8 * k + i for k, i in EDGE_TURNS))
        mid_turn = pick(t, tuple(8 * k + i for k, i in MID_TURNS))
        turn = jnp.where(edge, edge_turn, mid_turn)
        kind, i = turn // 8, turn % 8

        @pl.when(kind == 0)
        def _():
            take(i)

        @pl.when(t == 1)
        def _():
            for c in range(own):
                pan_t[c * width:(c + 1) * width, :] = pan[c].T

        @pl.when(kind == 1)
        def _():
            give(i)

        @pl.when(kind == 2)
        def _():
            forward(i)

        @pl.when(kind == 3)
        def _():
            pass_on(me + step, i, away)

    def tall(c):
        return jnp.concatenate([grads[b, q, c] for b, q in units], axis=0)

    def wide(lo, hi):
        return jnp.concatenate([rows_t[b, q, lo:hi] for b, q in units], axis=1)

    @pl.when(mid)
    def _():
        pass_on(me + 2 * step, 0, away)

    for j in range(keep):
        share_out[j] = jnp.dot(
            wide(split, half), tall((1 - dp) * keep + j), preferred_element_type=jnp.float32
        ).astype(jnp.bfloat16)
        share_copy(j).start()

    @pl.when(mid)
    def _():
        pass_on(me + 2 * step, 1, away)

    for j in range(keep):
        panel_out[j] = jnp.dot(
            wide(0, half), tall(dp * keep + j), preferred_element_type=jnp.float32
        )

    @pl.when(mid)
    def _():
        for p in range(2):
            pass_on(me + 2 * step, 2 + p, away)
            pass_on(me - step, p, home)

    @pl.loop(0, labs * CUTS)
    def _(u):
        off, cut = unit_of(u, edge)
        block = me + off * step
        twin_grads(block, cut).wait_recv()
        hand_over(core, block, cut).start()

    @pl.when(mid)
    def _():
        for p in range(2, pieces):
            pass_on(me + step, p, away)
            pass_on(me - step, p, home)

    for b, q in units:
        twin_rows(b, q).wait_recv()
        hand_over(1 - core, b, q).wait_recv()
    for j in range(keep):
        panel_out[j, :split] += jnp.dot(
            jnp.concatenate([twin_t[b, q] for b, q in units], axis=1),
            jnp.concatenate([twin_g[j, b, q] for b, q in units], axis=0),
            preferred_element_type=jnp.float32,
        )

    for q in range(CUTS):
        for i in range(PARTS):
            p = q * PARTS + i
            span = slice(i * piece, (i + 1) * piece)

            @pl.when(mid)
            def _():
                back_copy(me, p, away).wait_recv()
                held[me, q, span] += got[away, me, q, span].astype(jnp.float32)

            back_copy(me, p, home).wait_recv()
            enc_out[q, span] = (
                held[me, q, span] + got[home, me, q, span].astype(jnp.float32)
            ).astype(jnp.bfloat16)

    for j in range(keep):
        share_copy(j).wait_recv()
        panel_out[j, split:] += share_in[j].astype(jnp.float32)

    for off in range(1, labs):
        id_copy(off).wait_send()
    for j in range(keep):
        share_copy(j).wait_send()
    for block, cut in units:
        for w in range(WIDE):
            lx_copy(block, cut, w).wait_send()
        twin_rows(block, cut).wait_send()
        twin_grads(block, cut).wait_send()
        hand_over(core, block, cut).wait_send()
        off = (block - me) * step
        for p in range(cut * PARTS, (cut + 1) * PARTS):
            @pl.when((off == 0) | (mid & (off < 0)))
            def _():
                row_copy(block, p, away).wait_send()

            @pl.when(mid & (off >= 0))
            def _():
                row_copy(block, p, home).wait_send()

            @pl.when(off != 0)
            def _():
                back_copy(block, p, 0).wait_send()


def kernel_body(enc_rows, shortlist, cluster_slot, positives, panels):
    samples, half = enc_rows.shape
    own, _, width = panels.shape
    labs, dps = lax.axis_size("lab"), lax.axis_size("dp")
    beam, picks = shortlist.shape[1], positives.shape[1]
    size = samples // CUTS
    keep = own // dps
    split = half // 128 * 5 // 8 * 128
    f32, bf16 = jnp.float32, jnp.bfloat16
    vmem, dma = pltpu.VMEM, pltpu.SemaphoreType.DMA
    whole = pl.BlockSpec(memory_space=pltpu.VMEM)
    there = pl.BlockSpec(memory_space=pl.ANY)
    enc_grad, panel_grad = pl.pallas_call(
        functools.partial(
            step_kernel, (labs, dps, own, beam, picks, width, cluster_slot.shape[0])
        ),
        out_shape=(
            pltpu.VMEM((CUTS, size, half), bf16),
            pltpu.VMEM((keep, half, width), f32),
        ),
        in_specs=[there] * 5,
        out_specs=(whole, whole),
        scratch_shapes=[
            vmem((beam, samples), jnp.int32),
            vmem((picks, samples), jnp.int32),
            pltpu.SMEM(cluster_slot.shape, jnp.int32),
            vmem((labs, CUTS, size, half), bf16),
            vmem((labs, CUTS, half, size), bf16),
            vmem((labs, CUTS + 1, picks, size), jnp.int16),
            vmem((own, half, width), bf16),
            vmem((own * width, half), bf16),
            vmem((labs, CUTS, WIDE, size, own // WIDE * width), f32),
            vmem((labs, CUTS, WIDE, size, own // WIDE * width), f32),
            vmem((2, size, own * width), f32),
            vmem((labs, CUTS, own, size, width), bf16),
            vmem((labs, CUTS, size, half), f32),
            vmem((labs, CUTS, size, half), bf16),
            vmem((2, labs, CUTS, size, half), bf16),
            vmem((labs, CUTS, split, size), bf16),
            vmem((keep, labs, CUTS, size, width), bf16),
            vmem((keep, half - split, width), bf16),
            vmem((keep, half - split, width), bf16),
            dma((CUTS + own + 3,)),
            dma((2, labs, CUTS * PARTS)),
            dma((labs, CUTS * PARTS)),
            dma((labs,)),
            dma((labs,)),
            dma((labs, CUTS, WIDE)),
            dma((labs, CUTS, WIDE)),
            dma((labs, CUTS * PARTS)),
            dma((2, labs, CUTS * PARTS)),
            dma((labs, CUTS)),
            dma((labs, CUTS)),
            dma((labs, CUTS)),
            dma((labs, CUTS)),
            dma((labs, CUTS)),
            dma((labs, CUTS)),
            dma((keep,)),
            dma((keep,)),
        ],
        compiler_params=pltpu.CompilerParams(
            collective_id=0, has_side_effects=True, vmem_limit_bytes=56 << 20
        ),
    )(shortlist.T, positives.T, cluster_slot, enc_rows.reshape(CUTS, size, half), panels)
    return enc_grad.reshape(samples, half), panel_grad


def kernel_fits(enc_rows, shortlist, positives, panels):
    samples, half = enc_rows.shape
    own, _, width = panels.shape
    return (
        lax.axis_size("lab") == 4
        and lax.axis_size("dp") == 2
        and lax.axis_size("sub") == 2
        and own == 4
        and samples == CUTS * 128
        and half <= 1024
        and half % 256 == 0
        and width == 256
        and shortlist.shape[1] == 8
        and positives.shape[1] == 16
    )


def body(enc_rows, shortlist, cluster_slot, positives, panels):
    if kernel_fits(enc_rows, shortlist, positives, panels):
        return kernel_body(enc_rows, shortlist, cluster_slot, positives, panels)
    return array_body(enc_rows, shortlist, cluster_slot, positives, panels)


def solution(mesh):
    in_specs = (
        P(("grp", "lab", "dp"), "sub"),
        P(("grp", "lab", "dp"), None),
        P(),
        P(("grp", "lab", "dp"), None),
        P("lab", "sub", None),
    )
    out_specs = (P(("grp", "lab", "dp"), "sub"), P(("grp", "lab", "dp"), "sub", None))
    return jax.shard_map(body, mesh=mesh, in_specs=in_specs, out_specs=out_specs, check_vma=False)
```

```python
import functools

import jax
import jax.numpy as jnp
from jax import lax
from jax.experimental import pallas as pl
from jax.experimental.pallas import tpu as pltpu
from jax.sharding import PartitionSpec as P


def label_slots(shortlist, cluster_slot, positives, label_width):
    clusters = jnp.arange(cluster_slot.shape[0], dtype=jnp.int32)
    named = (shortlist[:, :, None] == clusters).astype(jnp.int32)
    slots = jnp.sum(named * cluster_slot, axis=2)
    beams = jnp.arange(shortlist.shape[1], dtype=jnp.int32)
    picked = (positives[:, :, None] // label_width == beams).astype(jnp.int32)
    pos_slot = jnp.sum(picked * slots[:, None, :], axis=2)
    return slots, pos_slot, positives % label_width


def array_body(enc_rows, shortlist, cluster_slot, positives, panels):
    samples, half = enc_rows.shape
    own, _, width = panels.shape
    labs = lax.axis_size("lab")
    slots, pos_slot, pos_col = label_slots(shortlist, cluster_slot, positives, width)
    ids = jnp.concatenate([slots, pos_slot * width + pos_col], axis=1)
    all_ids = lax.all_gather(ids, "lab", axis=0, tiled=True)
    all_rows = lax.all_gather(enc_rows, "lab", axis=0, tiled=True)
    beam = shortlist.shape[1]
    first = lax.axis_index("lab") * own
    columns = first * width + jnp.arange(own * width, dtype=jnp.int32)
    present = jnp.any(all_ids[:, :beam, None] == columns[None, None, :] // width, axis=1)
    target = jnp.any(all_ids[:, beam:, None] == columns[None, None, :], axis=1)
    flat = panels.transpose(1, 0, 2).reshape(half, own * width)
    partial = jnp.dot(all_rows, flat, preferred_element_type=jnp.float32)
    logits = lax.psum(partial, "sub")
    grad = jnp.where(present, jax.nn.sigmoid(logits) - target.astype(jnp.float32), 0.0)
    grad = grad.astype(jnp.bfloat16)
    back = lax.dot_general(
        grad, flat, (((1,), (1,)), ((), ())), preferred_element_type=jnp.float32
    ).astype(jnp.bfloat16)
    returned = lax.all_to_all(
        back.reshape(labs, samples, half), "lab", split_axis=0, concat_axis=0, tiled=True
    )
    enc_grad = jnp.sum(returned, axis=0, dtype=jnp.float32).astype(jnp.bfloat16)
    part = jnp.einsum(
        "rh,rcb->chb",
        all_rows,
        grad.reshape(labs * samples, own, width),
        preferred_element_type=jnp.float32,
    )
    panel_grad = lax.psum_scatter(part, "dp", scatter_dimension=0, tiled=True)
    return enc_grad, panel_grad


CUTS = 2
MESH = pl.DeviceIdType.MESH


def pick(u, values):
    out = jnp.int32(values[-1])
    for i in range(len(values) - 2, -1, -1):
        out = jnp.where(u == i, values[i], out)
    return out


EDGE_TURNS = (
    (0, 0), (0, 1), (1, 0), (1, 1), (0, 2), (1, 2), (0, 3), (1, 3),
    (0, 4), (1, 4), (0, 5), (1, 5), (0, 6), (1, 6), (0, 7), (1, 7),
)
MID_TURNS = (
    (0, 0), (0, 1), (2, 0), (1, 0), (2, 1), (1, 1), (0, 2), (0, 3), (2, 2), (1, 2), (1, 3), (2, 3), (0, 4), (0, 5), (2, 4), (1, 4), (1, 5), (2, 5), (0, 6), (2, 6), (1, 6), (3, 0), (2, 7), (0, 7), (3, 1), (1, 7),
)
PARTS = 2
WIDE = 2


def unit_of(u, edge):
    off = jnp.where(edge, pick(u, (0, 0, 1, 2, 3, 3, 2, 1)), pick(u, (0, 0, -1, 1, -1, 2, 2, 1)))
    cut = jnp.where(edge, pick(u, (0, 1, 0, 0, 0, 1, 1, 1)), pick(u, (0, 1, 0, 0, 1, 0, 1, 1)))
    return off, cut


def step_kernel(
    dims, short_hbm, pos_hbm, slot_hbm, enc_ref, panel_ref, enc_out, panel_out,
    short_ref, pos_ref, slot_ref,
    rows, rows_t, ids_buf, pan, pan_t, part, other, want, grads, held, sent, got,
    twin_t, twin_g, share_out, share_in,
    load_sem, row_send, row_recv, id_send, id_recv, lx_send, lx_recv, rt_send, rt_recv,
    tt_send, tt_recv, tg_send, tg_recv, fw_send, fw_recv, sh_send, sh_recv,
):
    labs, dps, own, beam, picks, width, clusters = dims
    half, size = rows_t.shape[2], rows_t.shape[3]
    keep = own // dps
    split = twin_t.shape[2]
    piece = size // PARTS
    pieces = CUTS * PARTS
    pair = own // WIDE
    me = lax.axis_index("lab")
    dp = lax.axis_index("dp")
    core = lax.axis_index("sub")
    edge = (me == 0) | (me == labs - 1)
    mid = jnp.logical_not(edge)
    low = me < labs // 2
    step = jnp.where(low, 1, -1)
    away = jnp.where(low, 1, 0)
    home = 1 - away
    units = [(b, q) for b in range(labs) for q in range(CUTS)]

    barrier = pltpu.get_barrier_semaphore()
    for off in range(1, labs):
        pl.semaphore_signal(barrier, inc=1, device_id={"lab": (me + off) % labs}, device_id_type=MESH)
    pl.semaphore_signal(barrier, inc=1, device_id={"dp": 1 - dp}, device_id_type=MESH)
    pl.semaphore_signal(barrier, inc=1, device_id={"sub": 1 - core}, device_id_type=MESH)

    loads = [
        pltpu.make_async_copy(enc_ref.at[q], rows.at[me, q], load_sem.at[q]) for q in range(CUTS)
    ] + [
        pltpu.make_async_copy(panel_ref.at[c], pan.at[c], load_sem.at[CUTS + c]) for c in range(own)
    ]
    small = [
        pltpu.make_async_copy(short_hbm, short_ref, load_sem.at[CUTS + own]),
        pltpu.make_async_copy(pos_hbm, pos_ref, load_sem.at[CUTS + own + 1]),
        pltpu.make_async_copy(slot_hbm, slot_ref, load_sem.at[CUTS + own + 2]),
    ]
    for load in small + loads:
        load.start()

    def remote(src, dst, send, recv, where):
        return pltpu.make_async_remote_copy(
            src_ref=src, dst_ref=dst, send_sem=send, recv_sem=recv,
            device_id=where, device_id_type=MESH,
        )

    def beside(side):
        return {"lab": jnp.clip(me + 2 * side - 1, 0, labs - 1)}

    def spot_of(p):
        return p // PARTS, pl.ds(pl.multiple_of((p % PARTS) * piece, piece), piece)

    def row_copy(block, p, side, src=None):
        cut, span = spot_of(p)
        here = rows.at[block, cut, span]
        return remote(
            here if src is None else src.at[cut, span], here,
            row_send.at[side, block, p], row_recv.at[block, p], beside(side),
        )

    def id_copy(off):
        return remote(
            ids_buf.at[me], ids_buf.at[me], id_send.at[off], id_recv.at[me], {"lab": (me + off) % labs}
        )

    def id_arrival(block):
        return remote(
            ids_buf.at[block], ids_buf.at[block], id_send.at[0], id_recv.at[block], beside(0)
        )

    def lx_copy(block, cut, w):
        return remote(
            part.at[block, cut, w], other.at[block, cut, w],
            lx_send.at[block, cut, w], lx_recv.at[block, cut, w], {"sub": 1 - core},
        )

    def back_copy(block, p, side):
        cut, span = spot_of(p)
        return remote(
            sent.at[block, cut, span], got.at[side, block, cut, span],
            rt_send.at[block, p], rt_recv.at[side, block, p], beside(side),
        )

    def twin_rows(block, cut):
        return remote(
            rows_t.at[block, cut, pl.ds(0, split)], twin_t.at[block, cut],
            tt_send.at[block, cut], tt_recv.at[block, cut], {"dp": 1 - dp},
        )

    def twin_grads(block, cut):
        return remote(
            grads.at[block, cut, (1 - dp) * keep + core], twin_g.at[core, block, cut],
            tg_send.at[block, cut], tg_recv.at[block, cut], {"dp": 1 - dp},
        )

    def hand_over(j, block, cut):
        return remote(
            twin_g.at[j, block, cut], twin_g.at[j, block, cut],
            fw_send.at[block, cut], fw_recv.at[block, cut], {"sub": 1 - core},
        )

    def share_copy(j):
        return remote(
            share_out.at[j], share_in.at[j], sh_send.at[j], sh_recv.at[j], {"dp": 1 - dp}
        )

    pl.semaphore_wait(barrier, labs + 1)

    for p in range(PARTS):
        row_copy(me, p, away, enc_ref).start()

        @pl.when(mid)
        def _():
            row_copy(me, p, home, enc_ref).start()

    for q in range(CUTS):
        loads[q].wait()
        rows_t[me, q] = rows[me, q].T
        twin_rows(me, q).start()
    for load in small:
        load.wait()
    short = short_ref[...]
    slots = jnp.zeros(short.shape, jnp.int32)
    for c in range(clusters):
        slots = jnp.where(short == c, slot_ref[c], slots)
    pos = pos_ref[...]
    spot = jnp.zeros(pos.shape, jnp.int32)
    for k in range(beam):
        local = pos - k * width
        spot = jnp.where((local >= 0) & (local < width), slots[k:k + 1] * width + local, spot)
    for q in range(CUTS):
        ids_buf[me, q] = spot[:, q * size:(q + 1) * size].astype(jnp.int16)
    ids_buf[me, CUTS] = jnp.concatenate(
        [slots[:, q * size:(q + 1) * size] for q in range(CUTS)], axis=0
    ).astype(jnp.int16)
    for off in range(1, labs):
        id_copy(off).start()

    @pl.when(edge)
    def _():
        for p in range(PARTS, pieces):
            row_copy(me, p, away, enc_ref).start()

    for load in loads[CUTS:]:
        load.wait()
    lane = lax.broadcasted_iota(jnp.int32, (1, width), 1).astype(jnp.float32)

    def forward(i):
        off = pick(i, (1, 1, 2, 2, 2, 2, 1, 1))
        p = pick(i, (0, 1, 0, 1, 2, 3, 2, 3))

        @pl.when(i < pieces)
        def _():
            row_copy(me - step, i, 0).wait_recv()
            row_copy(me - step, i, away).start()

        row_copy(me + off * step, p, 0).wait_recv()
        row_copy(me + off * step, p, home).start()

        @pl.when(i == pieces - 1)
        def _():
            for late in range(PARTS, pieces):
                row_copy(me, late, away, enc_ref).start()

        @pl.when(i == 2 * pieces - 1)
        def _():
            for late in range(PARTS, pieces):
                row_copy(me, late, home, enc_ref).start()

    def take(u):
        off, cut = unit_of(u, edge)
        block = me + off * step

        @pl.when(edge & (off != 0))
        def _():
            for i in range(PARTS):
                row_copy(block, cut * PARTS + i, 0).wait_recv()

        unit = rows[block, cut]
        for w in range(WIDE):
            for i in range(pair):
                part[block, cut, w, :, i * width:(i + 1) * width] = jnp.dot(
                    unit, pan[w * pair + i], preferred_element_type=jnp.float32
                )
            lx_copy(block, cut, w).start()

        @pl.when(off != 0)
        def _():
            rows_t[block, cut] = unit.T
            twin_rows(block, cut).start()

        @pl.when((off != 0) & (cut == 0))
        def _():
            id_arrival(block).wait_recv()

        spots = ids_buf[block, cut].astype(jnp.int32)
        named = ids_buf[block, CUTS].astype(jnp.int32)
        named = jnp.where(cut == 0, named[:beam], named[beam:])
        ids = jnp.concatenate([named, spots], axis=0).astype(jnp.float32)
        ids = jnp.concatenate([ids, jnp.zeros((128 - beam - picks, size), jnp.float32)], axis=0).T
        for c in range(own):
            slot = (me * own + c).astype(jnp.float32)
            present = jnp.zeros((size, 1), jnp.bool_)
            for k in range(beam):
                present = present | (ids[:, k:k + 1] == slot)
            here = lane + slot * width
            target = jnp.zeros((size, width), jnp.float32)
            for i in range(beam, beam + picks):
                target = jnp.where(ids[:, i:i + 1] == here, 1.0, target)
            want[u % 2, :, c * width:(c + 1) * width] = jnp.where(present, target, 2.0)

    def pass_on(block, p, side):
        cut, span = spot_of(p)
        back_copy(block, p, side).wait_recv()
        sent[block, cut, span] = (
            held[block, cut, span] + got[side, block, cut, span].astype(jnp.float32)
        ).astype(jnp.bfloat16)
        back_copy(block, p, side).start()

    def give(u):
        off, cut = unit_of(u, edge)
        block = me + off * step
        row = []
        for w in range(WIDE):
            lx_copy(block, cut, w).wait_recv()
            for i in range(pair):
                c = w * pair + i
                spread = slice(i * width, (i + 1) * width)
                logit = part[block, cut, w, :, spread] + other[block, cut, w, :, spread]
                goal = want[u % 2, :, c * width:(c + 1) * width]
                grad = jnp.where(goal > 1.5, 0.0, jax.nn.sigmoid(logit) - goal).astype(jnp.bfloat16)
                grads[block, cut, c] = grad
                row.append(grad)
        twin_grads(block, cut).start()
        total = jnp.dot(
            jnp.concatenate(row, axis=1), pan_t[...], preferred_element_type=jnp.float32
        )

        @pl.when(mid | (off == 0))
        def _():
            held[block, cut] = total

        @pl.when(edge & (off > 0))
        def _():
            sent[block, cut] = total.astype(jnp.bfloat16)
            for i in range(PARTS):
                back_copy(block, cut * PARTS + i, away).start()

    @pl.loop(0, jnp.where(edge, len(EDGE_TURNS), len(MID_TURNS)))
    def _(t):
        edge_turn = pick(t, tuple(8 * k + i for k, i in EDGE_TURNS))
        mid_turn = pick(t, tuple(8 * k + i for k, i in MID_TURNS))
        turn = jnp.where(edge, edge_turn, mid_turn)
        kind, i = turn // 8, turn % 8

        @pl.when(kind == 0)
        def _():
            take(i)

        @pl.when(t == 1)
        def _():
            for c in range(own):
                pan_t[c * width:(c + 1) * width, :] = pan[c].T

        @pl.when(kind == 1)
        def _():
            give(i)

        @pl.when(kind == 2)
        def _():
            forward(i)

        @pl.when(kind == 3)
        def _():
            pass_on(me + step, i, away)

    def tall(c):
        return jnp.concatenate([grads[b, q, c] for b, q in units], axis=0)

    def wide(lo, hi):
        return jnp.concatenate([rows_t[b, q, lo:hi] for b, q in units], axis=1)

    @pl.when(mid)
    def _():
        pass_on(me + 2 * step, 0, away)

    for j in range(keep):
        share_out[j] = jnp.dot(
            wide(split, half), tall((1 - dp) * keep + j), preferred_element_type=jnp.float32
        ).astype(jnp.bfloat16)
        share_copy(j).start()

    @pl.when(mid)
    def _():
        pass_on(me + 2 * step, 1, away)

    for j in range(keep):
        panel_out[j] = jnp.dot(
            wide(0, half), tall(dp * keep + j), preferred_element_type=jnp.float32
        )

    @pl.when(mid)
    def _():
        for p in range(2):
            pass_on(me + 2 * step, 2 + p, away)
            pass_on(me - step, p, home)

    @pl.loop(0, labs * CUTS)
    def _(u):
        off, cut = unit_of(u, edge)
        block = me + off * step
        twin_grads(block, cut).wait_recv()
        hand_over(core, block, cut).start()

    @pl.when(mid)
    def _():
        for p in range(2, pieces):
            pass_on(me + step, p, away)
            pass_on(me - step, p, home)

    for b, q in units:
        twin_rows(b, q).wait_recv()
        hand_over(1 - core, b, q).wait_recv()
    for j in range(keep):
        panel_out[j, :split] += jnp.dot(
            jnp.concatenate([twin_t[b, q] for b, q in units], axis=1),
            jnp.concatenate([twin_g[j, b, q] for b, q in units], axis=0),
            preferred_element_type=jnp.float32,
        )

    for off in range(1, labs):
        id_copy(off).wait_send()
    for block, cut in units:
        for w in range(WIDE):
            lx_copy(block, cut, w).wait_send()
        twin_rows(block, cut).wait_send()
        twin_grads(block, cut).wait_send()
        hand_over(core, block, cut).wait_send()
        off = (block - me) * step
        for p in range(cut * PARTS, (cut + 1) * PARTS):
            @pl.when((off == 0) | (mid & (off < 0)))
            def _():
                row_copy(block, p, away).wait_send()

            @pl.when(mid & (off >= 0))
            def _():
                row_copy(block, p, home).wait_send()

    for q in range(CUTS):
        for i in range(PARTS):
            p = q * PARTS + i
            span = slice(i * piece, (i + 1) * piece)

            @pl.when(mid)
            def _():
                back_copy(me, p, away).wait_recv()
                held[me, q, span] += got[away, me, q, span].astype(jnp.float32)

            back_copy(me, p, home).wait_recv()
            enc_out[q, span] = (
                held[me, q, span] + got[home, me, q, span].astype(jnp.float32)
            ).astype(jnp.bfloat16)

    for j in range(keep):
        share_copy(j).wait_recv()
        panel_out[j, split:] += share_in[j].astype(jnp.float32)

    for j in range(keep):
        share_copy(j).wait_send()
    for block, cut in units:
        for p in range(cut * PARTS, (cut + 1) * PARTS):
            @pl.when(block != me)
            def _():
                back_copy(block, p, 0).wait_send()


def store_kernel(enc_ref, panel_ref, enc_out, panel_out, sems):
    copies = [
        pltpu.make_async_copy(enc_ref, enc_out, sems.at[0]),
        pltpu.make_async_copy(panel_ref, panel_out, sems.at[1]),
    ]
    for copy in copies:
        copy.start()
    for copy in copies:
        copy.wait()


def kernel_body(enc_rows, shortlist, cluster_slot, positives, panels):
    samples, half = enc_rows.shape
    own, _, width = panels.shape
    labs, dps = lax.axis_size("lab"), lax.axis_size("dp")
    beam, picks = shortlist.shape[1], positives.shape[1]
    size = samples // CUTS
    keep = own // dps
    split = half * 45 // 64
    f32, bf16 = jnp.float32, jnp.bfloat16
    vmem, dma = pltpu.VMEM, pltpu.SemaphoreType.DMA
    whole = pl.BlockSpec(memory_space=pltpu.VMEM)
    there = pl.BlockSpec(memory_space=pl.ANY)
    enc_grad, panel_grad = pl.pallas_call(
        functools.partial(
            step_kernel, (labs, dps, own, beam, picks, width, cluster_slot.shape[0])
        ),
        out_shape=(
            pltpu.VMEM((CUTS, size, half), bf16),
            pltpu.VMEM((keep, half, width), f32),
        ),
        in_specs=[there] * 5,
        out_specs=(whole, whole),
        scratch_shapes=[
            vmem((beam, samples), jnp.int32),
            vmem((picks, samples), jnp.int32),
            pltpu.SMEM(cluster_slot.shape, jnp.int32),
            vmem((labs, CUTS, size, half), bf16),
            vmem((labs, CUTS, half, size), bf16),
            vmem((labs, CUTS + 1, picks, size), jnp.int16),
            vmem((own, half, width), bf16),
            vmem((own * width, half), bf16),
            vmem((labs, CUTS, WIDE, size, own // WIDE * width), f32),
            vmem((labs, CUTS, WIDE, size, own // WIDE * width), f32),
            vmem((2, size, own * width), f32),
            vmem((labs, CUTS, own, size, width), bf16),
            vmem((labs, CUTS, size, half), f32),
            vmem((labs, CUTS, size, half), bf16),
            vmem((2, labs, CUTS, size, half), bf16),
            vmem((labs, CUTS, split, size), bf16),
            vmem((keep, labs, CUTS, size, width), bf16),
            vmem((keep, half - split, width), bf16),
            vmem((keep, half - split, width), bf16),
            dma((CUTS + own + 3,)),
            dma((2, labs, CUTS * PARTS)),
            dma((labs, CUTS * PARTS)),
            dma((labs,)),
            dma((labs,)),
            dma((labs, CUTS, WIDE)),
            dma((labs, CUTS, WIDE)),
            dma((labs, CUTS * PARTS)),
            dma((2, labs, CUTS * PARTS)),
            dma((labs, CUTS)),
            dma((labs, CUTS)),
            dma((labs, CUTS)),
            dma((labs, CUTS)),
            dma((labs, CUTS)),
            dma((labs, CUTS)),
            dma((keep,)),
            dma((keep,)),
        ],
        compiler_params=pltpu.CompilerParams(
            collective_id=0, has_side_effects=True, vmem_limit_bytes=56 << 20
        ),
    )(shortlist.T, positives.T, cluster_slot, enc_rows.reshape(CUTS, size, half), panels)
    enc_grad, panel_grad = pl.pallas_call(
        store_kernel,
        out_shape=(
            jax.ShapeDtypeStruct(enc_grad.shape, bf16),
            jax.ShapeDtypeStruct(panel_grad.shape, f32),
        ),
        in_specs=[whole, whole],
        out_specs=(there, there),
        scratch_shapes=[dma((2,))],
    )(
        pltpu.with_memory_space_constraint(enc_grad, pltpu.VMEM),
        pltpu.with_memory_space_constraint(panel_grad, pltpu.VMEM),
    )
    return enc_grad.reshape(samples, half), panel_grad


def kernel_fits(enc_rows, shortlist, positives, panels):
    samples, half = enc_rows.shape
    own, _, width = panels.shape
    return (
        lax.axis_size("lab") == 4
        and lax.axis_size("dp") == 2
        and lax.axis_size("sub") == 2
        and own == 4
        and samples == CUTS * 128
        and half <= 1024
        and half % 256 == 0
        and width == 256
        and shortlist.shape[1] == 8
        and positives.shape[1] == 16
    )


def body(enc_rows, shortlist, cluster_slot, positives, panels):
    if kernel_fits(enc_rows, shortlist, positives, panels):
        return kernel_body(enc_rows, shortlist, cluster_slot, positives, panels)
    return array_body(enc_rows, shortlist, cluster_slot, positives, panels)


def solution(mesh):
    in_specs = (
        P(("grp", "lab", "dp"), "sub"),
        P(("grp", "lab", "dp"), None),
        P(),
        P(("grp", "lab", "dp"), None),
        P("lab", "sub", None),
    )
    out_specs = (P(("grp", "lab", "dp"), "sub"), P(("grp", "lab", "dp"), "sub", None))
    return jax.shard_map(body, mesh=mesh, in_specs=in_specs, out_specs=out_specs, check_vma=False)
```

```python
import functools

import jax
import jax.numpy as jnp
from jax import lax
from jax.experimental import pallas as pl
from jax.experimental.pallas import tpu as pltpu
from jax.sharding import PartitionSpec as P


def label_slots(shortlist, cluster_slot, positives, label_width):
    clusters = jnp.arange(cluster_slot.shape[0], dtype=jnp.int32)
    named = (shortlist[:, :, None] == clusters).astype(jnp.int32)
    slots = jnp.sum(named * cluster_slot, axis=2)
    beams = jnp.arange(shortlist.shape[1], dtype=jnp.int32)
    picked = (positives[:, :, None] // label_width == beams).astype(jnp.int32)
    pos_slot = jnp.sum(picked * slots[:, None, :], axis=2)
    return slots, pos_slot, positives % label_width


def array_body(enc_rows, shortlist, cluster_slot, positives, panels):
    samples, half = enc_rows.shape
    own, _, width = panels.shape
    labs = lax.axis_size("lab")
    slots, pos_slot, pos_col = label_slots(shortlist, cluster_slot, positives, width)
    ids = jnp.concatenate([slots, pos_slot * width + pos_col], axis=1)
    all_ids = lax.all_gather(ids, "lab", axis=0, tiled=True)
    all_rows = lax.all_gather(enc_rows, "lab", axis=0, tiled=True)
    beam = shortlist.shape[1]
    first = lax.axis_index("lab") * own
    columns = first * width + jnp.arange(own * width, dtype=jnp.int32)
    present = jnp.any(all_ids[:, :beam, None] == columns[None, None, :] // width, axis=1)
    target = jnp.any(all_ids[:, beam:, None] == columns[None, None, :], axis=1)
    flat = panels.transpose(1, 0, 2).reshape(half, own * width)
    partial = jnp.dot(all_rows, flat, preferred_element_type=jnp.float32)
    logits = lax.psum(partial, "sub")
    grad = jnp.where(present, jax.nn.sigmoid(logits) - target.astype(jnp.float32), 0.0)
    grad = grad.astype(jnp.bfloat16)
    back = lax.dot_general(
        grad, flat, (((1,), (1,)), ((), ())), preferred_element_type=jnp.float32
    ).astype(jnp.bfloat16)
    returned = lax.all_to_all(
        back.reshape(labs, samples, half), "lab", split_axis=0, concat_axis=0, tiled=True
    )
    enc_grad = jnp.sum(returned, axis=0, dtype=jnp.float32).astype(jnp.bfloat16)
    part = jnp.einsum(
        "rh,rcb->chb",
        all_rows,
        grad.reshape(labs * samples, own, width),
        preferred_element_type=jnp.float32,
    )
    panel_grad = lax.psum_scatter(part, "dp", scatter_dimension=0, tiled=True)
    return enc_grad, panel_grad


CUTS = 2
MESH = pl.DeviceIdType.MESH


def pick(u, values):
    out = jnp.int32(values[-1])
    for i in range(len(values) - 2, -1, -1):
        out = jnp.where(u == i, values[i], out)
    return out


EDGE_TURNS = (
    (0, 0), (0, 1), (1, 0), (1, 1), (0, 2), (1, 2), (0, 3), (1, 3),
    (0, 4), (1, 4), (0, 5), (1, 5), (0, 6), (1, 6), (0, 7), (1, 7),
)
MID_TURNS = (
    (0, 0), (0, 1), (2, 0), (1, 0), (2, 1), (1, 1), (0, 2), (0, 3), (2, 2), (1, 2), (1, 3), (2, 3), (0, 4), (0, 5), (2, 4), (1, 4), (1, 5), (2, 5), (0, 6), (2, 6), (1, 6), (3, 0), (2, 7), (0, 7), (3, 1), (1, 7),
)
PARTS = 2
WIDE = 2


def unit_of(u, edge):
    off = jnp.where(edge, pick(u, (0, 0, 1, 2, 3, 3, 2, 1)), pick(u, (0, 0, -1, 1, -1, 2, 2, 1)))
    cut = jnp.where(edge, pick(u, (0, 1, 0, 0, 0, 1, 1, 1)), pick(u, (0, 1, 0, 0, 1, 0, 1, 1)))
    return off, cut


def step_kernel(
    dims, short_hbm, pos_hbm, slot_hbm, enc_ref, panel_ref, enc_out, panel_out,
    short_ref, pos_ref, slot_ref,
    rows, rows_t, ids_buf, pan, pan_t, part, other, want, grads, held, sent, got,
    twin_t, twin_g, share_out, share_in,
    load_sem, row_send, row_recv, id_send, id_recv, lx_send, lx_recv, rt_send, rt_recv,
    tt_send, tt_recv, tg_send, tg_recv, fw_send, fw_recv, sh_send, sh_recv,
):
    labs, dps, own, beam, picks, width, clusters = dims
    half, size = rows_t.shape[2], rows_t.shape[3]
    keep = own // dps
    split = twin_t.shape[2]
    piece = size // PARTS
    pieces = CUTS * PARTS
    pair = own // WIDE
    me = lax.axis_index("lab")
    dp = lax.axis_index("dp")
    core = lax.axis_index("sub")
    edge = (me == 0) | (me == labs - 1)
    mid = jnp.logical_not(edge)
    low = me < labs // 2
    step = jnp.where(low, 1, -1)
    away = jnp.where(low, 1, 0)
    home = 1 - away
    units = [(b, q) for b in range(labs) for q in range(CUTS)]

    barrier = pltpu.get_barrier_semaphore()
    @pl.when(me > 0)
    def _():
        pl.semaphore_signal(barrier, inc=1, device_id={"lab": me - 1}, device_id_type=MESH)

    @pl.when(me < labs - 1)
    def _():
        pl.semaphore_signal(barrier, inc=1, device_id={"lab": me + 1}, device_id_type=MESH)

    pl.semaphore_signal(barrier, inc=1, device_id={"dp": 1 - dp}, device_id_type=MESH)
    pl.semaphore_signal(barrier, inc=1, device_id={"sub": 1 - core}, device_id_type=MESH)

    loads = [
        pltpu.make_async_copy(enc_ref.at[q], rows.at[me, q], load_sem.at[q]) for q in range(CUTS)
    ] + [
        pltpu.make_async_copy(panel_ref.at[c], pan.at[c], load_sem.at[CUTS + c]) for c in range(own)
    ]
    small = [
        pltpu.make_async_copy(short_hbm, short_ref, load_sem.at[CUTS + own]),
        pltpu.make_async_copy(pos_hbm, pos_ref, load_sem.at[CUTS + own + 1]),
        pltpu.make_async_copy(slot_hbm, slot_ref, load_sem.at[CUTS + own + 2]),
    ]
    for load in small + loads:
        load.start()

    def remote(src, dst, send, recv, where):
        return pltpu.make_async_remote_copy(
            src_ref=src, dst_ref=dst, send_sem=send, recv_sem=recv,
            device_id=where, device_id_type=MESH,
        )

    def beside(side):
        return {"lab": jnp.clip(me + 2 * side - 1, 0, labs - 1)}

    def spot_of(p):
        return p // PARTS, pl.ds(pl.multiple_of((p % PARTS) * piece, piece), piece)

    def row_copy(block, p, side, src=None):
        cut, span = spot_of(p)
        here = rows.at[block, cut, span]
        return remote(
            here if src is None else src.at[cut, span], here,
            row_send.at[side, block, p], row_recv.at[block, p], beside(side),
        )

    def id_copy(block, side):
        return remote(
            ids_buf.at[block], ids_buf.at[block],
            id_send.at[side, block], id_recv.at[block], beside(side),
        )

    def lx_copy(block, cut, w):
        return remote(
            part.at[block, cut, w], other.at[block, cut, w],
            lx_send.at[block, cut, w], lx_recv.at[block, cut, w], {"sub": 1 - core},
        )

    def back_copy(block, p, side):
        cut, span = spot_of(p)
        return remote(
            sent.at[block, cut, span], got.at[side, block, cut, span],
            rt_send.at[block, p], rt_recv.at[side, block, p], beside(side),
        )

    def twin_rows(block, cut):
        return remote(
            rows_t.at[block, cut, pl.ds(0, split)], twin_t.at[block, cut],
            tt_send.at[block, cut], tt_recv.at[block, cut], {"dp": 1 - dp},
        )

    def twin_grads(block, cut):
        return remote(
            grads.at[block, cut, (1 - dp) * keep + core], twin_g.at[core, block, cut],
            tg_send.at[block, cut], tg_recv.at[block, cut], {"dp": 1 - dp},
        )

    def hand_over(j, block, cut):
        return remote(
            twin_g.at[j, block, cut], twin_g.at[j, block, cut],
            fw_send.at[block, cut], fw_recv.at[block, cut], {"sub": 1 - core},
        )

    def share_copy(j):
        return remote(
            share_out.at[j], share_in.at[j], sh_send.at[j], sh_recv.at[j], {"dp": 1 - dp}
        )

    @pl.when(edge)
    def _():
        pl.semaphore_wait(barrier, 3)

    @pl.when(mid)
    def _():
        pl.semaphore_wait(barrier, 4)

    for p in range(PARTS):
        row_copy(me, p, away, enc_ref).start()

        @pl.when(mid)
        def _():
            row_copy(me, p, home, enc_ref).start()

    for q in range(CUTS):
        loads[q].wait()
        rows_t[me, q] = rows[me, q].T
        twin_rows(me, q).start()
    for load in small:
        load.wait()
    short = short_ref[...]
    slots = jnp.zeros(short.shape, jnp.int32)
    for c in range(clusters):
        slots = jnp.where(short == c, slot_ref[c], slots)
    pos = pos_ref[...]
    spot = jnp.zeros(pos.shape, jnp.int32)
    for k in range(beam):
        local = pos - k * width
        spot = jnp.where((local >= 0) & (local < width), slots[k:k + 1] * width + local, spot)
    for q in range(CUTS):
        ids_buf[me, q] = spot[:, q * size:(q + 1) * size].astype(jnp.int16)
    ids_buf[me, CUTS] = jnp.concatenate(
        [slots[:, q * size:(q + 1) * size] for q in range(CUTS)], axis=0
    ).astype(jnp.int16)
    id_copy(me, away).start()

    @pl.when(mid)
    def _():
        id_copy(me, home).start()

    @pl.when(edge)
    def _():
        for p in range(PARTS, pieces):
            row_copy(me, p, away, enc_ref).start()

    for load in loads[CUTS:]:
        load.wait()
    lane = lax.broadcasted_iota(jnp.int32, (1, width), 1).astype(jnp.float32)

    def forward(i):
        off = pick(i, (1, 1, 2, 2, 2, 2, 1, 1))
        p = pick(i, (0, 1, 0, 1, 2, 3, 2, 3))

        @pl.when(i < pieces)
        def _():
            row_copy(me - step, i, 0).wait_recv()
            row_copy(me - step, i, away).start()

        row_copy(me + off * step, p, 0).wait_recv()
        row_copy(me + off * step, p, home).start()

        @pl.when((i == 1) | (i == 3))
        def _():
            id_copy(me + off * step, 0).wait_recv()
            id_copy(me + off * step, home).start()

        @pl.when(i == 1)
        def _():
            id_copy(me - step, 0).wait_recv()
            id_copy(me - step, away).start()

        @pl.when(i == pieces - 1)
        def _():
            for late in range(PARTS, pieces):
                row_copy(me, late, away, enc_ref).start()

        @pl.when(i == 2 * pieces - 1)
        def _():
            for late in range(PARTS, pieces):
                row_copy(me, late, home, enc_ref).start()

    def take(u):
        off, cut = unit_of(u, edge)
        block = me + off * step

        @pl.when(edge & (off != 0))
        def _():
            for i in range(PARTS):
                row_copy(block, cut * PARTS + i, 0).wait_recv()

        unit = rows[block, cut]
        for w in range(WIDE):
            for i in range(pair):
                part[block, cut, w, :, i * width:(i + 1) * width] = jnp.dot(
                    unit, pan[w * pair + i], preferred_element_type=jnp.float32
                )
            lx_copy(block, cut, w).start()

        @pl.when(off != 0)
        def _():
            rows_t[block, cut] = unit.T
            twin_rows(block, cut).start()

        @pl.when(edge & (off != 0) & (cut == 0))
        def _():
            id_copy(block, 0).wait_recv()

        spots = ids_buf[block, cut].astype(jnp.int32)
        named = ids_buf[block, CUTS].astype(jnp.int32)
        named = jnp.where(cut == 0, named[:beam], named[beam:])
        ids = jnp.concatenate([named, spots], axis=0).astype(jnp.float32)
        ids = jnp.concatenate([ids, jnp.zeros((128 - beam - picks, size), jnp.float32)], axis=0).T
        for c in range(own):
            slot = (me * own + c).astype(jnp.float32)
            present = jnp.zeros((size, 1), jnp.bool_)
            for k in range(beam):
                present = present | (ids[:, k:k + 1] == slot)
            here = lane + slot * width
            target = jnp.zeros((size, width), jnp.float32)
            for i in range(beam, beam + picks):
                target = jnp.where(ids[:, i:i + 1] == here, 1.0, target)
            want[u % 2, :, c * width:(c + 1) * width] = jnp.where(present, target, 2.0)

    def pass_on(block, p, side):
        cut, span = spot_of(p)
        back_copy(block, p, side).wait_recv()
        sent[block, cut, span] = (
            held[block, cut, span] + got[side, block, cut, span].astype(jnp.float32)
        ).astype(jnp.bfloat16)
        back_copy(block, p, side).start()

    def give(u):
        off, cut = unit_of(u, edge)
        block = me + off * step
        row = []
        for w in range(WIDE):
            lx_copy(block, cut, w).wait_recv()
            for i in range(pair):
                c = w * pair + i
                spread = slice(i * width, (i + 1) * width)
                logit = part[block, cut, w, :, spread] + other[block, cut, w, :, spread]
                goal = want[u % 2, :, c * width:(c + 1) * width]
                grad = jnp.where(goal > 1.5, 0.0, jax.nn.sigmoid(logit) - goal).astype(jnp.bfloat16)
                grads[block, cut, c] = grad
                row.append(grad)
        twin_grads(block, cut).start()
        total = jnp.dot(
            jnp.concatenate(row, axis=1), pan_t[...], preferred_element_type=jnp.float32
        )

        @pl.when(mid | (off == 0))
        def _():
            held[block, cut] = total

        @pl.when(edge & (off > 0))
        def _():
            sent[block, cut] = total.astype(jnp.bfloat16)
            for i in range(PARTS):
                back_copy(block, cut * PARTS + i, away).start()

    @pl.loop(0, jnp.where(edge, len(EDGE_TURNS), len(MID_TURNS)))
    def _(t):
        edge_turn = pick(t, tuple(8 * k + i for k, i in EDGE_TURNS))
        mid_turn = pick(t, tuple(8 * k + i for k, i in MID_TURNS))
        turn = jnp.where(edge, edge_turn, mid_turn)
        kind, i = turn // 8, turn % 8

        @pl.when(kind == 0)
        def _():
            take(i)

        @pl.when(t == 1)
        def _():
            for c in range(own):
                pan_t[c * width:(c + 1) * width, :] = pan[c].T

        @pl.when(kind == 1)
        def _():
            give(i)

        @pl.when(kind == 2)
        def _():
            forward(i)

        @pl.when(kind == 3)
        def _():
            pass_on(me + step, i, away)

    def tall(c):
        return jnp.concatenate([grads[b, q, c] for b, q in units], axis=0)

    def wide(lo, hi):
        return jnp.concatenate([rows_t[b, q, lo:hi] for b, q in units], axis=1)

    @pl.when(mid)
    def _():
        pass_on(me + 2 * step, 0, away)

    for j in range(keep):
        share_out[j] = jnp.dot(
            wide(split, half), tall((1 - dp) * keep + j), preferred_element_type=jnp.float32
        ).astype(jnp.bfloat16)
        share_copy(j).start()

    @pl.when(mid)
    def _():
        pass_on(me + 2 * step, 1, away)

    for j in range(keep):
        panel_out[j] = jnp.dot(
            wide(0, half), tall(dp * keep + j), preferred_element_type=jnp.float32
        )

    @pl.when(mid)
    def _():
        for p in range(2):
            pass_on(me + 2 * step, 2 + p, away)
            pass_on(me - step, p, home)

    @pl.loop(0, labs * CUTS)
    def _(u):
        off, cut = unit_of(u, edge)
        block = me + off * step
        twin_grads(block, cut).wait_recv()
        hand_over(core, block, cut).start()

    @pl.when(mid)
    def _():
        for p in range(2, pieces):
            pass_on(me + step, p, away)
            pass_on(me - step, p, home)

    for b, q in units:
        twin_rows(b, q).wait_recv()
        hand_over(1 - core, b, q).wait_recv()
    for j in range(keep):
        panel_out[j, :split] += jnp.dot(
            jnp.concatenate([twin_t[b, q] for b, q in units], axis=1),
            jnp.concatenate([twin_g[j, b, q] for b, q in units], axis=0),
            preferred_element_type=jnp.float32,
        )

    for block in range(labs):
        off = (block - me) * step

        @pl.when((off == 0) | (mid & (off < 0)))
        def _():
            id_copy(block, away).wait_send()

        @pl.when(mid & (off >= 0))
        def _():
            id_copy(block, home).wait_send()

    for block, cut in units:
        for w in range(WIDE):
            lx_copy(block, cut, w).wait_send()
        twin_rows(block, cut).wait_send()
        twin_grads(block, cut).wait_send()
        hand_over(core, block, cut).wait_send()
        off = (block - me) * step
        for p in range(cut * PARTS, (cut + 1) * PARTS):
            @pl.when((off == 0) | (mid & (off < 0)))
            def _():
                row_copy(block, p, away).wait_send()

            @pl.when(mid & (off >= 0))
            def _():
                row_copy(block, p, home).wait_send()

    for q in range(CUTS):
        for i in range(PARTS):
            p = q * PARTS + i
            span = slice(i * piece, (i + 1) * piece)

            @pl.when(mid)
            def _():
                back_copy(me, p, away).wait_recv()
                held[me, q, span] += got[away, me, q, span].astype(jnp.float32)

            back_copy(me, p, home).wait_recv()
            enc_out[q, span] = (
                held[me, q, span] + got[home, me, q, span].astype(jnp.float32)
            ).astype(jnp.bfloat16)

    for j in range(keep):
        share_copy(j).wait_recv()
        panel_out[j, split:] += share_in[j].astype(jnp.float32)

    for j in range(keep):
        share_copy(j).wait_send()
    for block, cut in units:
        for p in range(cut * PARTS, (cut + 1) * PARTS):
            @pl.when(block != me)
            def _():
                back_copy(block, p, 0).wait_send()


def store_kernel(enc_ref, panel_ref, enc_out, panel_out, sems):
    copies = [
        pltpu.make_async_copy(enc_ref, enc_out, sems.at[0]),
        pltpu.make_async_copy(panel_ref, panel_out, sems.at[1]),
    ]
    for copy in copies:
        copy.start()
    for copy in copies:
        copy.wait()


def kernel_body(enc_rows, shortlist, cluster_slot, positives, panels):
    samples, half = enc_rows.shape
    own, _, width = panels.shape
    labs, dps = lax.axis_size("lab"), lax.axis_size("dp")
    beam, picks = shortlist.shape[1], positives.shape[1]
    size = samples // CUTS
    keep = own // dps
    split = half * 45 // 64
    f32, bf16 = jnp.float32, jnp.bfloat16
    vmem, dma = pltpu.VMEM, pltpu.SemaphoreType.DMA
    whole = pl.BlockSpec(memory_space=pltpu.VMEM)
    there = pl.BlockSpec(memory_space=pl.ANY)
    enc_grad, panel_grad = pl.pallas_call(
        functools.partial(
            step_kernel, (labs, dps, own, beam, picks, width, cluster_slot.shape[0])
        ),
        out_shape=(
            pltpu.VMEM((CUTS, size, half), bf16),
            pltpu.VMEM((keep, half, width), f32),
        ),
        in_specs=[there] * 5,
        out_specs=(whole, whole),
        scratch_shapes=[
            vmem((beam, samples), jnp.int32),
            vmem((picks, samples), jnp.int32),
            pltpu.SMEM(cluster_slot.shape, jnp.int32),
            vmem((labs, CUTS, size, half), bf16),
            vmem((labs, CUTS, half, size), bf16),
            vmem((labs, CUTS + 1, picks, size), jnp.int16),
            vmem((own, half, width), bf16),
            vmem((own * width, half), bf16),
            vmem((labs, CUTS, WIDE, size, own // WIDE * width), f32),
            vmem((labs, CUTS, WIDE, size, own // WIDE * width), f32),
            vmem((2, size, own * width), f32),
            vmem((labs, CUTS, own, size, width), bf16),
            vmem((labs, CUTS, size, half), f32),
            vmem((labs, CUTS, size, half), bf16),
            vmem((2, labs, CUTS, size, half), bf16),
            vmem((labs, CUTS, split, size), bf16),
            vmem((keep, labs, CUTS, size, width), bf16),
            vmem((keep, half - split, width), bf16),
            vmem((keep, half - split, width), bf16),
            dma((CUTS + own + 3,)),
            dma((2, labs, CUTS * PARTS)),
            dma((labs, CUTS * PARTS)),
            dma((2, labs)),
            dma((labs,)),
            dma((labs, CUTS, WIDE)),
            dma((labs, CUTS, WIDE)),
            dma((labs, CUTS * PARTS)),
            dma((2, labs, CUTS * PARTS)),
            dma((labs, CUTS)),
            dma((labs, CUTS)),
            dma((labs, CUTS)),
            dma((labs, CUTS)),
            dma((labs, CUTS)),
            dma((labs, CUTS)),
            dma((keep,)),
            dma((keep,)),
        ],
        compiler_params=pltpu.CompilerParams(
            collective_id=0, has_side_effects=True, vmem_limit_bytes=56 << 20
        ),
    )(shortlist.T, positives.T, cluster_slot, enc_rows.reshape(CUTS, size, half), panels)
    enc_grad, panel_grad = pl.pallas_call(
        store_kernel,
        out_shape=(
            jax.ShapeDtypeStruct(enc_grad.shape, bf16),
            jax.ShapeDtypeStruct(panel_grad.shape, f32),
        ),
        in_specs=[whole, whole],
        out_specs=(there, there),
        scratch_shapes=[dma((2,))],
    )(
        pltpu.with_memory_space_constraint(enc_grad, pltpu.VMEM),
        pltpu.with_memory_space_constraint(panel_grad, pltpu.VMEM),
    )
    return enc_grad.reshape(samples, half), panel_grad


def kernel_fits(enc_rows, shortlist, positives, panels):
    samples, half = enc_rows.shape
    own, _, width = panels.shape
    return (
        lax.axis_size("lab") == 4
        and lax.axis_size("dp") == 2
        and lax.axis_size("sub") == 2
        and own == 4
        and samples == CUTS * 128
        and half <= 1024
        and half % 256 == 0
        and width == 256
        and shortlist.shape[1] == 8
        and positives.shape[1] == 16
    )


def body(enc_rows, shortlist, cluster_slot, positives, panels):
    if kernel_fits(enc_rows, shortlist, positives, panels):
        return kernel_body(enc_rows, shortlist, cluster_slot, positives, panels)
    return array_body(enc_rows, shortlist, cluster_slot, positives, panels)


def solution(mesh):
    in_specs = (
        P(("grp", "lab", "dp"), "sub"),
        P(("grp", "lab", "dp"), None),
        P(),
        P(("grp", "lab", "dp"), None),
        P("lab", "sub", None),
    )
    out_specs = (P(("grp", "lab", "dp"), "sub"), P(("grp", "lab", "dp"), "sub", None))
    return jax.shard_map(body, mesh=mesh, in_specs=in_specs, out_specs=out_specs, check_vma=False)
```

```python
import functools

import jax
import jax.numpy as jnp
from jax import lax
from jax.experimental import pallas as pl
from jax.experimental.pallas import tpu as pltpu
from jax.sharding import PartitionSpec as P


def label_slots(shortlist, cluster_slot, positives, label_width):
    clusters = jnp.arange(cluster_slot.shape[0], dtype=jnp.int32)
    named = (shortlist[:, :, None] == clusters).astype(jnp.int32)
    slots = jnp.sum(named * cluster_slot, axis=2)
    beams = jnp.arange(shortlist.shape[1], dtype=jnp.int32)
    picked = (positives[:, :, None] // label_width == beams).astype(jnp.int32)
    pos_slot = jnp.sum(picked * slots[:, None, :], axis=2)
    return slots, pos_slot, positives % label_width


def array_body(enc_rows, shortlist, cluster_slot, positives, panels):
    samples, half = enc_rows.shape
    own, _, width = panels.shape
    labs = lax.axis_size("lab")
    slots, pos_slot, pos_col = label_slots(shortlist, cluster_slot, positives, width)
    ids = jnp.concatenate([slots, pos_slot * width + pos_col], axis=1)
    all_ids = lax.all_gather(ids, "lab", axis=0, tiled=True)
    all_rows = lax.all_gather(enc_rows, "lab", axis=0, tiled=True)
    beam = shortlist.shape[1]
    first = lax.axis_index("lab") * own
    columns = first * width + jnp.arange(own * width, dtype=jnp.int32)
    present = jnp.any(all_ids[:, :beam, None] == columns[None, None, :] // width, axis=1)
    target = jnp.any(all_ids[:, beam:, None] == columns[None, None, :], axis=1)
    flat = panels.transpose(1, 0, 2).reshape(half, own * width)
    partial = jnp.dot(all_rows, flat, preferred_element_type=jnp.float32)
    logits = lax.psum(partial, "sub")
    grad = jnp.where(present, jax.nn.sigmoid(logits) - target.astype(jnp.float32), 0.0)
    grad = grad.astype(jnp.bfloat16)
    back = lax.dot_general(
        grad, flat, (((1,), (1,)), ((), ())), preferred_element_type=jnp.float32
    ).astype(jnp.bfloat16)
    returned = lax.all_to_all(
        back.reshape(labs, samples, half), "lab", split_axis=0, concat_axis=0, tiled=True
    )
    enc_grad = jnp.sum(returned, axis=0, dtype=jnp.float32).astype(jnp.bfloat16)
    part = jnp.einsum(
        "rh,rcb->chb",
        all_rows,
        grad.reshape(labs * samples, own, width),
        preferred_element_type=jnp.float32,
    )
    panel_grad = lax.psum_scatter(part, "dp", scatter_dimension=0, tiled=True)
    return enc_grad, panel_grad


CUTS = 2
MESH = pl.DeviceIdType.MESH


def pick(u, values):
    out = jnp.int32(values[-1])
    for i in range(len(values) - 2, -1, -1):
        out = jnp.where(u == i, values[i], out)
    return out


EDGE_TURNS = (
    (0, 0), (0, 1), (1, 0), (1, 1), (0, 2), (1, 2), (0, 3), (1, 3),
    (0, 4), (1, 4), (0, 5), (1, 5), (0, 6), (1, 6), (0, 7), (1, 7),
)
MID_TURNS = (
    (0, 0), (0, 1), (2, 0), (1, 0), (2, 1), (1, 1), (0, 2), (0, 3), (2, 2), (1, 2), (1, 3), (2, 3), (0, 4), (0, 5), (2, 4), (1, 4), (1, 5), (2, 5), (0, 6), (2, 6), (1, 6), (3, 0), (2, 7), (0, 7), (3, 1), (1, 7),
)
PARTS = 2
WIDE = 2


def unit_of(u, edge):
    off = jnp.where(edge, pick(u, (0, 0, 1, 2, 3, 3, 2, 1)), pick(u, (0, 0, -1, 1, -1, 2, 2, 1)))
    cut = jnp.where(edge, pick(u, (0, 1, 0, 0, 0, 1, 1, 1)), pick(u, (0, 1, 0, 0, 1, 0, 1, 1)))
    return off, cut


def step_kernel(
    dims, short_hbm, pos_hbm, slot_hbm, enc_ref, panel_ref, enc_out, panel_out,
    short_ref, pos_ref, slot_ref,
    rows, rows_t, ids_buf, pan, pan_t, part, other, want, grads, held, sent, got,
    twin_t, twin_g, share_out, share_in,
    load_sem, row_send, row_recv, id_send, id_recv, lx_send, lx_recv, rt_send, rt_recv,
    tt_send, tt_recv, tg_send, tg_recv, fw_send, fw_recv, sh_send, sh_recv,
):
    labs, dps, own, beam, picks, width, clusters = dims
    half, size = rows_t.shape[2], rows_t.shape[3]
    keep = own // dps
    split = twin_t.shape[2]
    piece = size // PARTS
    pieces = CUTS * PARTS
    pair = own // WIDE
    me = lax.axis_index("lab")
    dp = lax.axis_index("dp")
    core = lax.axis_index("sub")
    edge = (me == 0) | (me == labs - 1)
    mid = jnp.logical_not(edge)
    low = me < labs // 2
    step = jnp.where(low, 1, -1)
    away = jnp.where(low, 1, 0)
    home = 1 - away
    units = [(b, q) for b in range(labs) for q in range(CUTS)]

    barrier = pltpu.get_barrier_semaphore()
    @pl.when(me > 0)
    def _():
        pl.semaphore_signal(barrier, inc=1, device_id={"lab": me - 1}, device_id_type=MESH)

    @pl.when(me < labs - 1)
    def _():
        pl.semaphore_signal(barrier, inc=1, device_id={"lab": me + 1}, device_id_type=MESH)

    pl.semaphore_signal(barrier, inc=1, device_id={"dp": 1 - dp}, device_id_type=MESH)
    pl.semaphore_signal(barrier, inc=1, device_id={"sub": 1 - core}, device_id_type=MESH)

    loads = [
        pltpu.make_async_copy(enc_ref.at[q], rows.at[me, q], load_sem.at[q]) for q in range(CUTS)
    ] + [
        pltpu.make_async_copy(panel_ref.at[c], pan.at[c], load_sem.at[CUTS + c]) for c in range(own)
    ]
    small = [
        pltpu.make_async_copy(short_hbm, short_ref, load_sem.at[CUTS + own]),
        pltpu.make_async_copy(pos_hbm, pos_ref, load_sem.at[CUTS + own + 1]),
        pltpu.make_async_copy(slot_hbm, slot_ref, load_sem.at[CUTS + own + 2]),
    ]
    for load in small + loads:
        load.start()

    def remote(src, dst, send, recv, where):
        return pltpu.make_async_remote_copy(
            src_ref=src, dst_ref=dst, send_sem=send, recv_sem=recv,
            device_id=where, device_id_type=MESH,
        )

    def beside(side):
        return {"lab": jnp.clip(me + 2 * side - 1, 0, labs - 1)}

    def spot_of(p):
        return p // PARTS, pl.ds(pl.multiple_of((p % PARTS) * piece, piece), piece)

    def row_copy(block, p, side, src=None):
        cut, span = spot_of(p)
        here = rows.at[block, cut, span]
        return remote(
            here if src is None else src.at[cut, span], here,
            row_send.at[side, block, p], row_recv.at[block, p], beside(side),
        )

    def id_copy(block, side):
        return remote(
            ids_buf.at[block], ids_buf.at[block],
            id_send.at[side, block], id_recv.at[block], beside(side),
        )

    def lx_copy(block, cut, w):
        return remote(
            part.at[block, cut, w], other.at[block, cut, w],
            lx_send.at[block, cut, w], lx_recv.at[block, cut, w], {"sub": 1 - core},
        )

    def back_copy(block, p, side):
        cut, span = spot_of(p)
        return remote(
            sent.at[block, cut, span], got.at[side, block, cut, span],
            rt_send.at[block, p], rt_recv.at[side, block, p], beside(side),
        )

    def twin_rows(block, cut):
        return remote(
            rows_t.at[block, cut, pl.ds(0, split)], twin_t.at[block, cut],
            tt_send.at[block, cut], tt_recv.at[block, cut], {"dp": 1 - dp},
        )

    def twin_grads(block, cut):
        return remote(
            grads.at[block, cut, (1 - dp) * keep + core], twin_g.at[core, block, cut],
            tg_send.at[block, cut], tg_recv.at[block, cut], {"dp": 1 - dp},
        )

    def hand_over(j, block, cut):
        return remote(
            twin_g.at[j, block, cut], twin_g.at[j, block, cut],
            fw_send.at[block, cut], fw_recv.at[block, cut], {"sub": 1 - core},
        )

    def share_copy(j):
        return remote(
            share_out.at[j], share_in.at[j], sh_send.at[j], sh_recv.at[j], {"dp": 1 - dp}
        )

    @pl.when(edge)
    def _():
        pl.semaphore_wait(barrier, 3)

    @pl.when(mid)
    def _():
        pl.semaphore_wait(barrier, 4)

    for p in range(PARTS):
        row_copy(me, p, away, enc_ref).start()

        @pl.when(mid)
        def _():
            row_copy(me, p, home, enc_ref).start()

    for q in range(CUTS):
        loads[q].wait()
        rows_t[me, q] = rows[me, q].T
        twin_rows(me, q).start()
    for load in small:
        load.wait()
    short = short_ref[...]
    slots = jnp.zeros(short.shape, jnp.int32)
    for c in range(clusters):
        slots = jnp.where(short == c, slot_ref[c], slots)
    pos = pos_ref[...]
    spot = jnp.zeros(pos.shape, jnp.int32)
    for k in range(beam):
        local = pos - k * width
        spot = jnp.where((local >= 0) & (local < width), slots[k:k + 1] * width + local, spot)
    for q in range(CUTS):
        ids_buf[me, q] = spot[:, q * size:(q + 1) * size].astype(jnp.int16)
    ids_buf[me, CUTS] = jnp.concatenate(
        [slots[:, q * size:(q + 1) * size] for q in range(CUTS)], axis=0
    ).astype(jnp.int16)
    id_copy(me, away).start()

    @pl.when(mid)
    def _():
        id_copy(me, home).start()

    @pl.when(edge)
    def _():
        for p in range(PARTS, pieces):
            row_copy(me, p, away, enc_ref).start()

    for load in loads[CUTS:]:
        load.wait()
    lane = lax.broadcasted_iota(jnp.int32, (1, width), 1).astype(jnp.float32)

    def forward(i):
        off = pick(i, (1, 1, 2, 2, 2, 2, 1, 1))
        p = pick(i, (0, 1, 0, 1, 2, 3, 2, 3))

        @pl.when(i < pieces)
        def _():
            row_copy(me - step, i, 0).wait_recv()
            row_copy(me - step, i, away).start()

        row_copy(me + off * step, p, 0).wait_recv()
        row_copy(me + off * step, p, home).start()

        @pl.when((i == 1) | (i == 3))
        def _():
            id_copy(me + off * step, 0).wait_recv()
            id_copy(me + off * step, home).start()

        @pl.when(i == 1)
        def _():
            id_copy(me - step, 0).wait_recv()
            id_copy(me - step, away).start()

        @pl.when(i == pieces - 1)
        def _():
            for late in range(PARTS, pieces):
                row_copy(me, late, away, enc_ref).start()

        @pl.when(i == 2 * pieces - 1)
        def _():
            for late in range(PARTS, pieces):
                row_copy(me, late, home, enc_ref).start()

    def take(u):
        off, cut = unit_of(u, edge)
        block = me + off * step

        @pl.when(edge & (off != 0))
        def _():
            for i in range(PARTS):
                row_copy(block, cut * PARTS + i, 0).wait_recv()

        unit = rows[block, cut]
        for w in range(WIDE):
            for i in range(pair):
                part[block, cut, w, :, i * width:(i + 1) * width] = jnp.dot(
                    unit, pan[w * pair + i], preferred_element_type=jnp.float32
                )
            lx_copy(block, cut, w).start()

        @pl.when(off != 0)
        def _():
            rows_t[block, cut] = unit.T
            twin_rows(block, cut).start()

        @pl.when(edge & (off != 0) & (cut == 0))
        def _():
            id_copy(block, 0).wait_recv()

        spots = ids_buf[block, cut].astype(jnp.int32)
        named = ids_buf[block, CUTS].astype(jnp.int32)
        named = jnp.where(cut == 0, named[:beam], named[beam:])
        ids = jnp.concatenate([named, spots], axis=0).astype(jnp.float32)
        ids = jnp.concatenate([ids, jnp.zeros((128 - beam - picks, size), jnp.float32)], axis=0).T
        for c in range(own):
            slot = (me * own + c).astype(jnp.float32)
            present = jnp.zeros((size, 1), jnp.bool_)
            for k in range(beam):
                present = present | (ids[:, k:k + 1] == slot)
            here = lane + slot * width
            target = jnp.zeros((size, width), jnp.float32)
            for i in range(beam, beam + picks):
                target = jnp.where(ids[:, i:i + 1] == here, 1.0, target)
            want[u % 2, :, c * width:(c + 1) * width] = jnp.where(present, target, 2.0)

    def pass_on(block, p, side):
        cut, span = spot_of(p)
        back_copy(block, p, side).wait_recv()
        sent[block, cut, span] = (
            held[block, cut, span] + got[side, block, cut, span].astype(jnp.float32)
        ).astype(jnp.bfloat16)
        back_copy(block, p, side).start()

    def tall(c):
        return jnp.concatenate([grads[b, q, c] for b, q in units], axis=0)

    def wide(lo, hi):
        return jnp.concatenate([rows_t[b, q, lo:hi] for b, q in units], axis=1)

    def give(u):
        off, cut = unit_of(u, edge)
        block = me + off * step
        row = []
        for w in range(WIDE):
            lx_copy(block, cut, w).wait_recv()
            for i in range(pair):
                c = w * pair + i
                spread = slice(i * width, (i + 1) * width)
                logit = part[block, cut, w, :, spread] + other[block, cut, w, :, spread]
                goal = want[u % 2, :, c * width:(c + 1) * width]
                grad = jnp.where(goal > 1.5, 0.0, jax.nn.sigmoid(logit) - goal).astype(jnp.bfloat16)
                grads[block, cut, c] = grad
                row.append(grad)
        twin_grads(block, cut).start()

        @pl.when(u == labs * CUTS - 1)
        def _():
            for j in range(keep):
                share_out[j] = jnp.dot(
                    wide(split, half), tall((1 - dp) * keep + j), preferred_element_type=jnp.float32
                ).astype(jnp.bfloat16)
                share_copy(j).start()

        total = jnp.dot(
            jnp.concatenate(row, axis=1), pan_t[...], preferred_element_type=jnp.float32
        )

        @pl.when(mid | (off == 0))
        def _():
            held[block, cut] = total

        @pl.when(edge & (off > 0))
        def _():
            sent[block, cut] = total.astype(jnp.bfloat16)
            for i in range(PARTS):
                back_copy(block, cut * PARTS + i, away).start()

    @pl.loop(0, jnp.where(edge, len(EDGE_TURNS), len(MID_TURNS)))
    def _(t):
        edge_turn = pick(t, tuple(8 * k + i for k, i in EDGE_TURNS))
        mid_turn = pick(t, tuple(8 * k + i for k, i in MID_TURNS))
        turn = jnp.where(edge, edge_turn, mid_turn)
        kind, i = turn // 8, turn % 8

        @pl.when(kind == 0)
        def _():
            take(i)

        @pl.when(t == 1)
        def _():
            for c in range(own):
                pan_t[c * width:(c + 1) * width, :] = pan[c].T

        @pl.when(kind == 1)
        def _():
            give(i)

        @pl.when(kind == 2)
        def _():
            forward(i)

        @pl.when(kind == 3)
        def _():
            pass_on(me + step, i, away)

    @pl.when(mid)
    def _():
        pass_on(me + 2 * step, 0, away)

    @pl.when(mid)
    def _():
        pass_on(me + 2 * step, 1, away)

    for j in range(keep):
        panel_out[j] = jnp.dot(
            wide(0, half), tall(dp * keep + j), preferred_element_type=jnp.float32
        )

    @pl.when(mid)
    def _():
        for p in range(2):
            pass_on(me + 2 * step, 2 + p, away)
            pass_on(me - step, p, home)

    @pl.when(mid)
    def _():
        for p in range(2, pieces):
            pass_on(me + step, p, away)
            pass_on(me - step, p, home)

    @pl.loop(0, labs * CUTS)
    def _(u):
        off, cut = unit_of(u, edge)
        block = me + off * step
        twin_grads(block, cut).wait_recv()
        hand_over(core, block, cut).start()

    for b, q in units:
        twin_rows(b, q).wait_recv()
        hand_over(1 - core, b, q).wait_recv()
    for j in range(keep):
        panel_out[j, :split] += jnp.dot(
            jnp.concatenate([twin_t[b, q] for b, q in units], axis=1),
            jnp.concatenate([twin_g[j, b, q] for b, q in units], axis=0),
            preferred_element_type=jnp.float32,
        )

    for block in range(labs):
        off = (block - me) * step

        @pl.when((off == 0) | (mid & (off < 0)))
        def _():
            id_copy(block, away).wait_send()

        @pl.when(mid & (off >= 0))
        def _():
            id_copy(block, home).wait_send()

    for block, cut in units:
        for w in range(WIDE):
            lx_copy(block, cut, w).wait_send()
        twin_rows(block, cut).wait_send()
        twin_grads(block, cut).wait_send()
        hand_over(core, block, cut).wait_send()
        off = (block - me) * step
        for p in range(cut * PARTS, (cut + 1) * PARTS):
            @pl.when((off == 0) | (mid & (off < 0)))
            def _():
                row_copy(block, p, away).wait_send()

            @pl.when(mid & (off >= 0))
            def _():
                row_copy(block, p, home).wait_send()

    for q in range(CUTS):
        for i in range(PARTS):
            p = q * PARTS + i
            span = slice(i * piece, (i + 1) * piece)

            @pl.when(mid)
            def _():
                back_copy(me, p, away).wait_recv()
                held[me, q, span] += got[away, me, q, span].astype(jnp.float32)

            back_copy(me, p, home).wait_recv()
            enc_out[q, span] = (
                held[me, q, span] + got[home, me, q, span].astype(jnp.float32)
            ).astype(jnp.bfloat16)

    for block, cut in units:
        for p in range(cut * PARTS, (cut + 1) * PARTS):
            @pl.when(block != me)
            def _():
                back_copy(block, p, 0).wait_send()

    for j in range(keep):
        share_copy(j).wait_recv()
        panel_out[j, split:] += share_in[j].astype(jnp.float32)
        share_copy(j).wait_send()


def store_kernel(enc_ref, panel_ref, enc_out, panel_out, sems):
    copies = [
        pltpu.make_async_copy(enc_ref, enc_out, sems.at[0]),
        pltpu.make_async_copy(panel_ref, panel_out, sems.at[1]),
    ]
    for copy in copies:
        copy.start()
    for copy in copies:
        copy.wait()


def kernel_body(enc_rows, shortlist, cluster_slot, positives, panels):
    samples, half = enc_rows.shape
    own, _, width = panels.shape
    labs, dps = lax.axis_size("lab"), lax.axis_size("dp")
    beam, picks = shortlist.shape[1], positives.shape[1]
    size = samples // CUTS
    keep = own // dps
    split = half * 45 // 64
    f32, bf16 = jnp.float32, jnp.bfloat16
    vmem, dma = pltpu.VMEM, pltpu.SemaphoreType.DMA
    whole = pl.BlockSpec(memory_space=pltpu.VMEM)
    there = pl.BlockSpec(memory_space=pl.ANY)
    enc_grad, panel_grad = pl.pallas_call(
        functools.partial(
            step_kernel, (labs, dps, own, beam, picks, width, cluster_slot.shape[0])
        ),
        out_shape=(
            pltpu.VMEM((CUTS, size, half), bf16),
            pltpu.VMEM((keep, half, width), f32),
        ),
        in_specs=[there] * 5,
        out_specs=(whole, whole),
        scratch_shapes=[
            vmem((beam, samples), jnp.int32),
            vmem((picks, samples), jnp.int32),
            pltpu.SMEM(cluster_slot.shape, jnp.int32),
            vmem((labs, CUTS, size, half), bf16),
            vmem((labs, CUTS, half, size), bf16),
            vmem((labs, CUTS + 1, picks, size), jnp.int16),
            vmem((own, half, width), bf16),
            vmem((own * width, half), bf16),
            vmem((labs, CUTS, WIDE, size, own // WIDE * width), f32),
            vmem((labs, CUTS, WIDE, size, own // WIDE * width), f32),
            vmem((2, size, own * width), f32),
            vmem((labs, CUTS, own, size, width), bf16),
            vmem((labs, CUTS, size, half), f32),
            vmem((labs, CUTS, size, half), bf16),
            vmem((2, labs, CUTS, size, half), bf16),
            vmem((labs, CUTS, split, size), bf16),
            vmem((keep, labs, CUTS, size, width), bf16),
            vmem((keep, half - split, width), bf16),
            vmem((keep, half - split, width), bf16),
            dma((CUTS + own + 3,)),
            dma((2, labs, CUTS * PARTS)),
            dma((labs, CUTS * PARTS)),
            dma((2, labs)),
            dma((labs,)),
            dma((labs, CUTS, WIDE)),
            dma((labs, CUTS, WIDE)),
            dma((labs, CUTS * PARTS)),
            dma((2, labs, CUTS * PARTS)),
            dma((labs, CUTS)),
            dma((labs, CUTS)),
            dma((labs, CUTS)),
            dma((labs, CUTS)),
            dma((labs, CUTS)),
            dma((labs, CUTS)),
            dma((keep,)),
            dma((keep,)),
        ],
        compiler_params=pltpu.CompilerParams(
            collective_id=0, has_side_effects=True, vmem_limit_bytes=56 << 20
        ),
    )(shortlist.T, positives.T, cluster_slot, enc_rows.reshape(CUTS, size, half), panels)
    enc_grad, panel_grad = pl.pallas_call(
        store_kernel,
        out_shape=(
            jax.ShapeDtypeStruct(enc_grad.shape, bf16),
            jax.ShapeDtypeStruct(panel_grad.shape, f32),
        ),
        in_specs=[whole, whole],
        out_specs=(there, there),
        scratch_shapes=[dma((2,))],
    )(
        pltpu.with_memory_space_constraint(enc_grad, pltpu.VMEM),
        pltpu.with_memory_space_constraint(panel_grad, pltpu.VMEM),
    )
    return enc_grad.reshape(samples, half), panel_grad


def kernel_fits(enc_rows, shortlist, positives, panels):
    samples, half = enc_rows.shape
    own, _, width = panels.shape
    return (
        lax.axis_size("lab") == 4
        and lax.axis_size("dp") == 2
        and lax.axis_size("sub") == 2
        and own == 4
        and samples == CUTS * 128
        and half <= 1024
        and half % 256 == 0
        and width == 256
        and shortlist.shape[1] == 8
        and positives.shape[1] == 16
    )


def body(enc_rows, shortlist, cluster_slot, positives, panels):
    if kernel_fits(enc_rows, shortlist, positives, panels):
        return kernel_body(enc_rows, shortlist, cluster_slot, positives, panels)
    return array_body(enc_rows, shortlist, cluster_slot, positives, panels)


def solution(mesh):
    in_specs = (
        P(("grp", "lab", "dp"), "sub"),
        P(("grp", "lab", "dp"), None),
        P(),
        P(("grp", "lab", "dp"), None),
        P("lab", "sub", None),
    )
    out_specs = (P(("grp", "lab", "dp"), "sub"), P(("grp", "lab", "dp"), "sub", None))
    return jax.shard_map(body, mesh=mesh, in_specs=in_specs, out_specs=out_specs, check_vma=False)
```
